32 devices in a mesh: gx: 4 (over x, core), gy: 8 (over z, y).
Axes of the slice: x: 2, y: 2, z: 4, core: 2. Of those that a mesh axis runs over, the one named last changes fastest.
Arguments:
- samples: bfloat16 [64, 128, 32, 256], P('gx', 'gy'), may hold values from -6 to 6
- leaf_basis: bfloat16 [64, 256], replicated, may hold values from -0.375 to 0.375
- transfer: bfloat16 [5, 64, 256], replicated, may hold values from -0.5 to 0.5
- coupling: bfloat16 [5, 7, 64, 448], replicated, may hold values from -0.15625 to 0.15625
- near_tiles: bfloat16 [9, 256, 256], replicated, may hold values from -0.125 to 0.125
- codes_local: int32 [64, 128, 4, 27], P('gx', 'gy'), may hold values from 0 to 35, as said below
- counts_local: int32 [64, 128, 4], P('gx', 'gy'), may hold values from 1 to 27, as said below
- codes_upper: int32 [40, 27], replicated, may hold values from 0 to 35, as said below
- counts_upper: int32 [40], replicated, may hold values from 1 to 27, as said below
Outputs:
- response: bfloat16 [64, 128, 32, 256], P('gx', 'gy')
The draws below stay inside these ranges and needn't reach their ends.
Inputs may be any that keep to these rules, and one draw needn't show every extreme that they name: `codes_local`: entries [i, j, l, :] with i and j multiples of 2^l hold the list of the level-l cluster whose first leaf is (i, j); other entries are not read. Its first count entries are distinct codes a * 6 + b of clusters more than one step away from the target in some direction. `counts_local`: length of the list stored at the same position. `codes_upper`: row n is the list of the n-th cluster of level 4 and coarser, levels in order from 4, row-major within a level, each level with half the rows and columns of the one before and the last with 2 rows; first count entries distinct codes of clusters more than one step away from the target in some direction. `counts_upper`: length of the list of the same row.
All inputs are finite; a program needn't handle non-finite values.
Results may differ from the reference program's by a relative error of at most 0.0095.
Values may be sent and summed in bfloat16 or wider, within the bound.
A program may use at most 384 MiB of HBM per device.

```python
import jax
import jax.numpy as jnp
import numpy as np
from jax import lax

LEAF = 256
R = 64
NV = 32
LOCAL = 4
LISTMAX = 27
PATCH = 16
NXL = 64
NYL = 128
UPPER = 40


def near_flags(row_bits, col_bits):
    code_ids = jnp.arange(36, dtype=jnp.int32)
    code_row = code_ids // 6
    code_col = code_ids % 6
    return (code_row >= 1 + row_bits[..., None]) & (code_row <= 3 + row_bits[..., None]) & (code_col >= 1 + col_bits[..., None]) & (code_col <= 3 + col_bits[..., None])


def draw_lists(key, row_bits, col_bits):
    full_shape = row_bits.shape + (36,)
    code_ids = jnp.arange(36, dtype=jnp.int32)
    scores = jax.random.randint(key, full_shape, 0, 2 ** 20, dtype=jnp.int32) * 64 + code_ids
    scores = jnp.where(near_flags(row_bits, col_bits), 2 ** 30 + code_ids, scores)
    ordering = jnp.argsort(scores, axis=-1, stable=True)
    return ordering[..., :LISTMAX].astype(jnp.int32)


def local_bits():
    level_scale = jnp.asarray([2 ** level_index for level_index in range(LOCAL)], jnp.int32)
    leaf_row = jnp.arange(NXL, dtype=jnp.int32)[:, None, None]
    leaf_col = jnp.arange(NYL, dtype=jnp.int32)[None, :, None]
    row_bits = jnp.broadcast_to(leaf_row // level_scale % 2, (NXL, NYL, LOCAL))
    col_bits = jnp.broadcast_to(leaf_col // level_scale % 2, (NXL, NYL, LOCAL))
    return (row_bits, col_bits)


def upper_positions():
    row_list = []
    col_list = []
    grid_rows = NXL // PATCH
    grid_cols = NYL // PATCH
    while grid_rows >= 2:
        row_list.append(np.repeat(np.arange(grid_rows), grid_cols))
        col_list.append(np.tile(np.arange(grid_cols), grid_rows))
        grid_rows = grid_rows // 2
        grid_cols = grid_cols // 2
    return (np.concatenate(row_list), np.concatenate(col_list))


def draw_codes_local(key, part):
    row_bits, col_bits = local_bits()
    return draw_lists(jax.random.fold_in(key, 11), row_bits, col_bits)


def draw_counts_local(key, part):
    heat_level = jax.random.randint(jax.random.fold_in(key, 21), (NXL // PATCH, NYL // PATCH, LOCAL), 1, 5, dtype=jnp.int32)
    heat_level = jnp.repeat(jnp.repeat(heat_level, PATCH, axis=0), PATCH, axis=1)
    base_count = jax.random.randint(jax.random.fold_in(key, 22), (NXL, NYL, LOCAL), 0, LISTMAX, dtype=jnp.int32)
    return (1 + base_count * heat_level // 4).astype(jnp.int32)


def draw_codes_upper(key, part):
    row_list, col_list = upper_positions()
    row_bits = jnp.asarray(row_list % 2, jnp.int32)
    col_bits = jnp.asarray(col_list % 2, jnp.int32)
    return draw_lists(jax.random.fold_in(key, 31), row_bits, col_bits)


def draw_counts_upper(key, part):
    heat_level = jax.random.randint(jax.random.fold_in(key, 41), (UPPER,), 1, 5, dtype=jnp.int32)
    base_count = jax.random.randint(jax.random.fold_in(key, 42), (UPPER,), 0, LISTMAX, dtype=jnp.int32)
    return (1 + base_count * heat_level // 4).astype(jnp.int32)


def shard_levels(own_key, extent, shards, least, high):
    loudness, own = 1.0, jax.random.fold_in(own_key, 6)
    for position, shards_of in shards:
        steps = jnp.exp(jax.random.uniform(jax.random.fold_in(own, position), (shards_of,), jnp.float32, least / len(shards), high / len(shards)))
        loudness = loudness * jnp.repeat(steps, extent[position] // shards_of).reshape([-1 if axis == position else 1 for axis in range(len(extent))])
    return loudness


def gaussian(own_key, extent, width, most, pieces=(), kind=jnp.bfloat16):
    gain = shard_levels(own_key, extent, pieces, -0.22, 0.18) if pieces else 1.0
    values = jax.random.normal(own_key, extent, jnp.float32) * width * gain
    return jnp.minimum(jnp.maximum(values, -most), most).astype(kind)


def setup_inputs(seed: int = 0) -> dict:
    splits = jax.random.split(jax.random.key(seed), 10)
    samples = gaussian(splits[0], (NXL, NYL, NV, LEAF), 1.0, 6.0, ((0, 4), (1, 8)))
    leaf_basis = gaussian(splits[1], (R, LEAF), LEAF ** -0.5, 0.375)
    transfer = gaussian(splits[2], (LOCAL + 1, R, 4 * R), (2 * R) ** -0.5, 0.5)
    coupling = gaussian(splits[3], (LOCAL + 1, 7, R, 7 * R), (27 * R) ** -0.5, 0.15625)
    near_tiles = gaussian(splits[4], (9, LEAF, LEAF), (9 * LEAF) ** -0.5, 0.125)
    codes_local = draw_codes_local(jax.random.fold_in(splits[9], 71), 0)
    counts_local = draw_counts_local(jax.random.fold_in(splits[9], 71), 0)
    codes_upper = draw_codes_upper(jax.random.fold_in(splits[9], 71), 0)
    counts_upper = draw_counts_upper(jax.random.fold_in(splits[9], 71), 0)
    return dict(samples=samples, leaf_basis=leaf_basis, transfer=transfer, coupling=coupling, near_tiles=near_tiles, codes_local=codes_local, counts_local=counts_local, codes_upper=codes_upper, counts_upper=counts_upper)


def is_near(row_step, col_step):
    return abs(row_step) <= 1 and abs(col_step) <= 1


def lift_level(children, matrices):
    grid_rows, grid_cols, vectors, rank_size = children.shape
    grouped = children.reshape(grid_rows // 2, 2, grid_cols // 2, 2, vectors, rank_size)
    grouped = grouped.transpose(0, 2, 4, 1, 3, 5).reshape(grid_rows // 2, grid_cols // 2, vectors, 4 * rank_size)
    parent = jnp.einsum('pqvc,sc->pqvs', grouped.astype(jnp.float32), matrices.astype(jnp.float32))
    return parent.astype(jnp.bfloat16)


def spread(parent, matrices):
    grid_rows, grid_cols, vectors, rank_size = parent.shape
    carried = jnp.einsum('pqvs,sc->pqvc', parent.astype(jnp.float32), matrices.astype(jnp.float32))
    carried = carried.reshape(grid_rows, grid_cols, vectors, 2, 2, rank_size).transpose(0, 3, 1, 4, 2, 5)
    return carried.reshape(2 * grid_rows, 2 * grid_cols, vectors, rank_size)


def member_table(list_codes, counts):
    slot_index = jnp.arange(list_codes.shape[-1], dtype=jnp.int32)
    active = slot_index < counts[..., None]
    matches = (list_codes[..., None] == jnp.arange(36, dtype=jnp.int32)) & active[..., None]
    return jnp.any(matches, axis=-2).astype(jnp.float32)


def couple(padded, member, matrices):
    grid_rows = padded.shape[0] - 4
    grid_cols = padded.shape[1] - 4
    vectors = padded.shape[2]
    rank_size = padded.shape[3]
    member = member.reshape(grid_rows // 2, 2, grid_cols // 2, 2, 36)
    totals = [[jnp.zeros((grid_rows // 2, grid_cols // 2, vectors, rank_size), jnp.float32) for col_bit in range(2)] for row_bit in range(2)]
    for code_row in range(6):
        for code_col in range(6):
            parities = [(row_bit, col_bit) for row_bit in range(2) for col_bit in range(2) if not is_near(code_row - 2 - row_bit, code_col - 2 - col_bit)]
            if not parities:
                continue
            source = padded[code_row:code_row + grid_rows:2, code_col:code_col + grid_cols:2]
            blocks = jnp.concatenate([matrices[code_row + 1 - row_bit, :, (code_col + 1 - col_bit) * rank_size:(code_col + 2 - col_bit) * rank_size] for (row_bit, col_bit) in parities], axis=0)
            images = jnp.einsum('pqvr,sr->pqvs', source.astype(jnp.float32), blocks.astype(jnp.float32))
            for number, (row_bit, col_bit) in enumerate(parities):
                weight_mask = member[:, row_bit, :, col_bit, code_row * 6 + code_col]
                totals[row_bit][col_bit] = totals[row_bit][col_bit] + weight_mask[..., None, None] * images[..., number * rank_size:(number + 1) * rank_size]
    stacked = jnp.stack([jnp.stack(totals[row_bit], axis=0) for row_bit in range(2)], axis=0)
    return stacked.transpose(2, 0, 3, 1, 4, 5).reshape(grid_rows, grid_cols, vectors, rank_size)


def reference(samples, leaf_basis, transfer, coupling, near_tiles, codes_local, counts_local, codes_upper, counts_upper):
    leaf_rows = samples.shape[0]
    leaf_cols = samples.shape[1]
    row_blocks = leaf_rows // PATCH
    blocked = samples.reshape(row_blocks, PATCH, leaf_cols, NV, LEAF)

    def project(rows_block):
        return jnp.einsum('ijvs,rs->ijvr', rows_block.astype(jnp.float32), leaf_basis.astype(jnp.float32)).astype(jnp.bfloat16)

    level_coeffs = [lax.map(project, blocked).reshape(leaf_rows, leaf_cols, NV, R)]
    while level_coeffs[-1].shape[0] > 2:
        level_index = len(level_coeffs) - 1
        level_coeffs.append(lift_level(level_coeffs[-1], transfer[min(level_index, LOCAL)]))

    members = []
    offset = 0
    for level_index, coeffs in enumerate(level_coeffs):
        if level_index < LOCAL:
            stride = 2 ** level_index
            members.append(member_table(codes_local[::stride, ::stride, level_index], counts_local[::stride, ::stride, level_index]))
        else:
            grid_rows = coeffs.shape[0]
            grid_cols = coeffs.shape[1]
            count_here = grid_rows * grid_cols
            members.append(member_table(codes_upper[offset:offset + count_here].reshape(grid_rows, grid_cols, LISTMAX), counts_upper[offset:offset + count_here].reshape(grid_rows, grid_cols)))
            offset = offset + count_here

    images = []
    for level_index, coeffs in enumerate(level_coeffs):
        padded = jnp.pad(coeffs, ((2, 2), (2, 2), (0, 0), (0, 0)))
        images.append(couple(padded, members[level_index], coupling[min(level_index, LOCAL)]))
    downward = images[-1]
    for level_index in range(len(level_coeffs) - 2, -1, -1):
        downward = images[level_index] + spread(downward.astype(jnp.bfloat16), transfer[min(level_index, LOCAL)])

    padded_samples = jnp.pad(samples, ((1, 1), (1, 1), (0, 0), (0, 0)))
    far_coeffs = downward.astype(jnp.bfloat16).reshape(row_blocks, PATCH, leaf_cols, NV, R)

    def finish(inputs):
        block_index, coeffs = inputs
        window = lax.dynamic_slice_in_dim(padded_samples, block_index * PATCH, PATCH + 2, 0)
        summed = jnp.einsum('ijvr,rs->ijvs', coeffs.astype(jnp.float32), leaf_basis.astype(jnp.float32))
        for step_row in range(3):
            for step_col in range(3):
                neighbour = window[step_row:step_row + PATCH, step_col:step_col + leaf_cols]
                summed = summed + jnp.einsum('ijvs,ts->ijvt', neighbour.astype(jnp.float32), near_tiles[step_row * 3 + step_col].astype(jnp.float32))
        return summed.astype(jnp.bfloat16)

    result = lax.map(finish, (jnp.arange(row_blocks, dtype=jnp.int32), far_coeffs))
    return result.reshape(leaf_rows, leaf_cols, NV, LEAF)
```

```python
import functools

import jax
import jax.numpy as jnp
from jax import lax
from jax.experimental import pallas as pl
from jax.experimental.pallas import tpu as pltpu
from jax.sharding import PartitionSpec as P

MESH = pl.DeviceIdType.MESH
F32 = jnp.float32
BF16 = jnp.bfloat16
NT = (((1,), (1,)), ((), ()))
NN = (((1,), (0,)), ((), ()))
VMEM_LIMIT = 60 * 1024 * 1024
AXES = ("gx", "gy")
SIDES = [(sx, sy) for sx in (-1, 0, 1) for sy in (-1, 0, 1) if (sx, sy) != (0, 0)]


def dot(a, b, dims):
    return lax.dot_general(a, b, dims, preferred_element_type=F32)


def twice(matrix):
    return jnp.concatenate([matrix, matrix], axis=0)


def low_half(shape, rank):
    return lax.broadcasted_iota(jnp.int32, shape, len(shape) - 1) < rank


def pair_columns(wide, vectors, rank):
    pairs = wide.reshape(-1, 2, vectors, 2 * rank)
    even, odd = pairs[:, 0], pairs[:, 1]
    return jnp.where(low_half(even.shape, rank), even, odd).astype(BF16)


def split_columns(paired, rank):
    count, vectors, lanes = paired.shape
    low = low_half((1, lanes), rank).astype(F32).astype(BF16)
    both = jnp.stack([paired * low, paired * (1 - low)], axis=1)
    return both.reshape(count * 2 * vectors, lanes)


def up_kernel(levels, rank, samples, basis, transfer, *outs):
    patch, _, vectors, sources = samples.shape
    basis2 = twice(basis[...])

    def project(i, carry):
        rows = samples[i].reshape(patch * vectors, sources)
        outs[0][i] = pair_columns(dot(rows, basis2, NT), vectors, rank)
        return carry

    lax.fori_loop(0, patch, project, 0)
    for level in range(levels):
        child = outs[level]
        matrix = twice(transfer[level])
        for row in range(child.shape[0] // 2):
            grouped = jnp.concatenate([child[2 * row], child[2 * row + 1]], axis=-1)
            wide = dot(grouped.reshape(-1, 4 * rank), matrix, NT)
            if level < levels - 1:
                outs[level + 1][row] = pair_columns(wide, vectors, rank)
            else:
                odd = lax.axis_index("gy") % 2
                lane = lax.broadcasted_iota(jnp.int32, wide.shape, 1)
                own = (lane >= odd * rank) & (lane < (odd + 1) * rank)
                outs[level + 1][...] = jnp.where(own, wide, 0.0).astype(BF16)


def span(side, size, width):
    if side == 0:
        return pl.ds(0, size), pl.ds(width, size)
    if side > 0:
        return pl.ds(size - width, width), pl.ds(0, width)
    return pl.ds(0, width), pl.ds(width + size, width)


def exchange_kernel(widths, counts, *refs):
    blocks = len(widths)
    ins, top = refs[:blocks], refs[blocks]
    outs, top_out = refs[blocks + 1 : 2 * blocks + 1], refs[2 * blocks + 1]
    send, recv, local, top_send, top_recv = refs[2 * blocks + 2 :]
    across, along = counts
    total = across * along
    row, col = lax.axis_index("gx"), lax.axis_index("gy")
    me = row * along + col

    def place(device):
        return (device // along, device % along)

    barrier = pltpu.get_barrier_semaphore()

    def greet(step, carry):
        pl.semaphore_signal(
            barrier, inc=1, device_id=place((me + step) % total), device_id_type=MESH
        )
        return carry

    lax.fori_loop(1, total, greet, 0)
    pl.semaphore_wait(barrier, total - 1)

    def top_copy(step):
        return pltpu.make_async_remote_copy(
            src_ref=top,
            dst_ref=top_out.at[row, col],
            send_sem=top_send.at[step],
            recv_sem=top_recv.at[step],
            device_id=place((me + step) % total),
            device_id_type=MESH,
        )

    def start_top(step, carry):
        top_copy(step).start()
        return carry

    def side_copy(block, number):
        sx, sy = SIDES[number]
        source, target = ins[block], outs[block]
        wx, wy = widths[block]
        rows_from, rows_to = span(sx, source.shape[0], wx)
        cols_from, cols_to = span(sy, source.shape[1], wy)
        return pltpu.make_async_remote_copy(
            src_ref=source.at[rows_from, cols_from],
            dst_ref=target.at[rows_to, cols_to],
            send_sem=send.at[block, number],
            recv_sem=recv.at[block, number],
            device_id=(row + sx, col + sy),
            device_id_type=MESH,
        )

    def land(block, number):
        sx, sy = SIDES[number]
        source, target = ins[block], outs[block]
        wx, wy = widths[block]
        rows_from, rows_to = span(sx, source.shape[0], wx)
        cols_from, cols_to = span(sy, source.shape[1], wy)
        return pltpu.make_async_remote_copy(
            src_ref=source.at[rows_from, cols_from],
            dst_ref=target.at[rows_to, cols_to],
            send_sem=send.at[block, number],
            recv_sem=recv.at[block, number],
            device_id=(row - sx, col - sy),
            device_id_type=MESH,
        )

    def inside(sx, sy):
        there_row, there_col = row + sx, col + sy
        return (there_row >= 0) & (there_row < across) & (there_col >= 0) & (there_col < along)

    lax.fori_loop(1, total, start_top, 0)
    for number, (sx, sy) in enumerate(SIDES):

        @pl.when(inside(sx, sy))
        def _():
            for block in range(blocks):
                side_copy(block, number).start()

    own = []
    for block in range(blocks):
        wx, wy = widths[block]
        size_x, size_y = ins[block].shape[:2]
        copy = pltpu.make_async_copy(
            ins[block],
            outs[block].at[pl.ds(wx, size_x), pl.ds(wy, size_y)],
            local.at[block],
        )
        copy.start()
        own.append(copy)
    own_top = pltpu.make_async_copy(top, top_out.at[row, col], local.at[blocks])
    own_top.start()
    for copy in own:
        copy.wait()
    own_top.wait()
    for number, (sx, sy) in enumerate(SIDES):

        @pl.when(inside(-sx, -sy))
        def _():
            for block in range(blocks):
                land(block, number).wait_recv()

    def wait_top(step, carry):
        sender = (me + total - step) % total
        came = pltpu.make_async_remote_copy(
            src_ref=top,
            dst_ref=top_out.at[sender // along, sender % along],
            send_sem=top_send.at[step],
            recv_sem=top_recv.at[step],
            device_id=place(sender),
            device_id_type=MESH,
        )
        came.wait_recv()
        return carry

    lax.fori_loop(1, total, wait_top, 0)
    for block in range(blocks):
        target = outs[block]
        wx, wy = widths[block]
        rows, cols = target.shape[:2]
        for edge, spot in (
            (row == 0, (pl.ds(0, wx), pl.ds(0, cols))),
            (row == across - 1, (pl.ds(rows - wx, wx), pl.ds(0, cols))),
            (col == 0, (pl.ds(0, rows), pl.ds(0, wy))),
            (col == along - 1, (pl.ds(0, rows), pl.ds(cols - wy, wy))),
        ):

            @pl.when(edge)
            def _():
                shape = (spot[0].size, spot[1].size) + target.shape[2:]
                target[spot[0], spot[1]] = jnp.zeros(shape, target.dtype)

    for number, (sx, sy) in enumerate(SIDES):

        @pl.when(inside(sx, sy))
        def _():
            for block in range(blocks):
                side_copy(block, number).wait_send()

    def sent_top(step, carry):
        top_copy(step).wait_send()
        return carry

    lax.fori_loop(1, total, sent_top, 0)


def main_kernel(levels, rank, steps, offsets, *refs):
    padded_samples = refs[0]
    padded = refs[1 : 1 + levels]
    (tops, codes, codes_upper, basis, transfer, coupling, shifted, near, out) = refs[
        1 + levels : 10 + levels
    ]
    scratch = refs[10 + levels :]
    codes_flat, masks = scratch[0], scratch[1]
    uppers = scratch[2 : 2 + steps]
    downs = scratch[2 + steps :]
    patch, _, vectors, sources = out.shape
    across, along = tops.shape[:2]
    lanes = 2 * rank
    wide = 36 * rank
    row_index, col_index = lax.axis_index("gx"), lax.axis_index("gy")

    for level in range(levels):
        size = patch >> level
        for row in range(size):
            begin = (row << level) * patch * levels + level
            codes_flat[offsets[level] + row * size : offsets[level] + (row + 1) * size, :] = codes[
                pl.ds(begin, size, stride=levels << level), :
            ]
    codes_flat[offsets[levels] : offsets[levels] + codes_upper.shape[0], :] = codes_upper[...]
    code_lane = lax.broadcasted_iota(jnp.int32, (128, wide), 1) // rank
    code_row = lax.broadcasted_iota(jnp.int32, (128, wide), 0)
    widen = (code_lane == code_row).astype(F32).astype(BF16)
    group = 64

    def member(number, carry):
        start = pl.multiple_of(number * group, group)
        listed = codes_flat[pl.ds(start, group), :]
        code = lax.broadcasted_iota(jnp.int32, (group, 128), 1)
        found = jnp.zeros((group, 128), F32)
        for slot in range(listed.shape[1]):
            found = jnp.where(listed[:, slot : slot + 1] == code, 1.0, found)
        masks[pl.ds(start, group), :] = dot(found.astype(BF16), widen, NN)
        return carry

    lax.fori_loop(0, masks.shape[0] // group, member, 0)

    def weights(level, row_bit, col_bit):
        source = coupling if col_bit else shifted
        flat = jnp.concatenate(
            [source[level, code + 1 - row_bit, :, 0 : 6 * rank] for code in range(6)], axis=-1
        )
        return twice(flat)

    def window(ref, row, col):
        return jnp.concatenate(
            [ref[row + code, col + step] for code in range(6) for step in range(3)], axis=-1
        )

    def masked(slab, mask_row):
        mask = jnp.broadcast_to(masks[pl.ds(mask_row, 1), :], (16, wide)).astype(BF16)
        return (slab.reshape(-1, 16, wide) * mask[None]).reshape(slab.shape)

    uppers[0][...] = jnp.zeros(uppers[0].shape, BF16)
    for row in range(across):
        for col in range(along // 2):
            uppers[0][row + 2, col + 1] = tops[row, 2 * col] + tops[row, 2 * col + 1]
    top_matrix = twice(transfer[levels])
    for step in range(steps - 1):
        child, parent = uppers[step], uppers[step + 1]
        parent[...] = jnp.zeros(parent.shape, BF16)
        rows, cols = across >> step, along >> (step + 1)
        for row in range(rows // 2):
            grouped = jnp.concatenate(
                [child[2 * row + 2, 1 : 1 + cols], child[2 * row + 3, 1 : 1 + cols]], axis=-1
            )
            lifted = dot(grouped.reshape(-1, 4 * rank), top_matrix, NT)
            parent[row + 2, 1 : 1 + cols // 2] = pair_columns(lifted, vectors, rank)
    low = low_half((vectors, lanes), rank)
    low_mask = low_half((1, lanes), rank).astype(F32).astype(BF16)
    images = []
    begin = offsets[levels]
    for step in range(steps):
        rows, cols = across >> step, along >> step
        row, col = row_index // 2**step, col_index // 2**step
        slab = window(uppers[step], 2 * (row // 2), col // 2)
        slab = masked(slab, begin + row * cols + col)
        bit = row % 2
        image = []
        for source in (shifted, coupling):
            flat = jnp.concatenate(
                [source[levels, code + 1 - bit, :, 0 : 6 * rank] for code in range(6)], axis=-1
            )
            image.append(dot(slab, twice(flat), NT))
        images.append(jnp.where(col % 2 == 0, image[0], image[1]))
        begin += rows * cols
    down = images[-1]
    for step in range(steps - 2, -1, -1):
        row, col = row_index // 2**step, col_index // 2**step
        carried = dot(down.astype(BF16) * low_mask, top_matrix, NN)
        part = jnp.where(row % 2 == 0, carried[:, :lanes], carried[:, lanes:])
        turned = pltpu.roll(part, rank, 1)
        part = jnp.where(low == (col % 2 == 0), part, turned)
        down = images[step] + part
    spread_top = down.astype(BF16) * low_mask

    def level_row(level, row):
        size = patch >> level
        if level == levels - 1:
            parent = spread_top
        else:
            parent = split_columns(downs[level + 1][row], rank)
        carried = dot(parent, twice(transfer[level]), NN)
        slabs = [window(padded[level], 2 * row, col) for col in range(size // 2)]
        for row_bit in range(2):
            image = []
            for col_bit in range(2):
                start = offsets[level] + (2 * row + row_bit) * size + col_bit
                left = jnp.concatenate(
                    [masked(slabs[col], start + 2 * col) for col in range(size // 2)], axis=0
                )
                image.append(dot(left, weights(level, row_bit, col_bit), NT))
            total = jnp.where(low_half(image[0].shape, rank), image[0], image[1])
            total = total + carried[:, row_bit * lanes : (row_bit + 1) * lanes]
            downs[level][2 * row + row_bit] = total.astype(BF16).reshape(-1, vectors, lanes)

    for level in range(levels - 1, -1, -1):
        count = patch >> (level + 1)
        if count <= 2:
            for row in range(count):
                level_row(level, row)
        else:

            def body(row, carry, level=level):
                level_row(level, row)
                return carry

            lax.fori_loop(0, count, body, 0)

    near_flat = jnp.concatenate([near[number] for number in range(9)], axis=-1)
    basis2 = twice(basis[...])

    def finish(row, carry):
        left = jnp.concatenate(
            [
                padded_samples[row + step_row, step_col : step_col + patch].reshape(-1, sources)
                for step_row in range(3)
                for step_col in range(3)
            ],
            axis=-1,
        )
        total = dot(left, near_flat, NT)
        total = total + dot(split_columns(downs[0][row], rank), basis2, NN)
        out[row] = total.astype(BF16).reshape(patch, vectors, sources)
        return carry

    lax.fori_loop(0, patch, finish, 0)


def shards(
    samples,
    leaf_basis,
    transfer,
    coupling,
    near_tiles,
    codes_local,
    counts_local,
    codes_upper,
    counts_upper,
):
    patch, _, vectors, sources = samples.shape
    rank = leaf_basis.shape[0]
    levels = transfer.shape[0] - 1
    lanes = 2 * rank
    across, along = lax.axis_size("gx"), lax.axis_size("gy")
    steps = 1
    while across >> steps >= 2:
        steps += 1
    vmem = pl.BlockSpec(memory_space=pltpu.VMEM)

    slot = jnp.arange(codes_local.shape[-1], dtype=jnp.int32)
    listed = jnp.where(slot < counts_local[..., None], codes_local, -1)
    listed = listed.reshape(-1, codes_local.shape[-1])
    listed_upper = jnp.where(slot < counts_upper[..., None], codes_upper, -1)

    shapes = [
        jax.ShapeDtypeStruct((patch >> level, patch >> (level + 1), vectors, lanes), BF16)
        for level in range(levels)
    ]
    shapes.append(jax.ShapeDtypeStruct((vectors, lanes), BF16))
    coeffs = pl.pallas_call(
        functools.partial(up_kernel, levels, rank),
        out_shape=shapes,
        in_specs=[vmem] * 3,
        out_specs=[vmem] * len(shapes),
        compiler_params=pltpu.CompilerParams(vmem_limit_bytes=VMEM_LIMIT),
        name="up",
    )(samples, leaf_basis, transfer)

    blocks = [samples, *coeffs[:levels]]
    widths = [(1, 1)] + [(2, 1)] * levels
    padded_shapes = [
        jax.ShapeDtypeStruct(
            (block.shape[0] + 2 * wx, block.shape[1] + 2 * wy) + block.shape[2:], BF16
        )
        for block, (wx, wy) in zip(blocks, widths)
    ]
    padded_shapes.append(jax.ShapeDtypeStruct((across, along, vectors, lanes), BF16))
    total = across * along
    padded = pl.pallas_call(
        functools.partial(exchange_kernel, widths, (across, along)),
        out_shape=padded_shapes,
        in_specs=[vmem] * (len(blocks) + 1),
        out_specs=[vmem] * len(padded_shapes),
        scratch_shapes=[
            pltpu.SemaphoreType.DMA((len(blocks), len(SIDES))),
            pltpu.SemaphoreType.DMA((len(blocks), len(SIDES))),
            pltpu.SemaphoreType.DMA((len(blocks) + 1,)),
            pltpu.SemaphoreType.DMA((total,)),
            pltpu.SemaphoreType.DMA((total,)),
        ],
        compiler_params=pltpu.CompilerParams(
            collective_id=0, has_side_effects=True, vmem_limit_bytes=VMEM_LIMIT
        ),
        name="exchange",
    )(*blocks, coeffs[levels])

    offsets = [0]
    for level in range(levels):
        offsets.append(offsets[-1] + (patch >> level) ** 2)
    rows = offsets[-1] + codes_upper.shape[0]
    rows = (rows + 63) // 64 * 64
    shifted = coupling[..., rank:]
    return pl.pallas_call(
        functools.partial(main_kernel, levels, rank, steps, offsets),
        out_shape=jax.ShapeDtypeStruct(samples.shape, BF16),
        in_specs=[vmem] * (levels + 9),
        out_specs=vmem,
        scratch_shapes=[
            pltpu.VMEM((rows, codes_local.shape[-1]), jnp.int32),
            pltpu.VMEM((rows, 36 * rank), F32),
        ]
        + [
            pltpu.VMEM(((across >> step) + 4, (along >> (step + 1)) + 2, vectors, lanes), BF16)
            for step in range(steps)
        ]
        + [pltpu.VMEM(shape.shape, BF16) for shape in shapes[:levels]],
        compiler_params=pltpu.CompilerParams(vmem_limit_bytes=VMEM_LIMIT),
        name="finish",
    )(*padded, listed, listed_upper, leaf_basis, transfer, coupling, shifted, near_tiles)


def solution(mesh):
    placed = (
        P("gx", "gy", None, None),
        P(),
        P(),
        P(),
        P(),
        P("gx", "gy", None, None),
        P("gx", "gy", None),
        P(),
        P(),
    )
    return jax.shard_map(
        shards, mesh=mesh, in_specs=placed, out_specs=P("gx", "gy", None, None), check_vma=False
    )
```

```python
import functools

import jax
import jax.numpy as jnp
from jax import lax
from jax.experimental import pallas as pl
from jax.experimental.pallas import tpu as pltpu
from jax.sharding import PartitionSpec as P

MESH = pl.DeviceIdType.MESH
F32 = jnp.float32
BF16 = jnp.bfloat16
NT = (((1,), (1,)), ((), ()))
NN = (((1,), (0,)), ((), ()))
VMEM_LIMIT = 60 * 1024 * 1024
AXES = ("gx", "gy")
SIDES = [(sx, sy) for sx in (-1, 0, 1) for sy in (-1, 0, 1) if (sx, sy) != (0, 0)]


def dot(a, b, dims):
    return lax.dot_general(a, b, dims, preferred_element_type=F32)


def twice(matrix):
    return jnp.concatenate([matrix, matrix], axis=0)


def low_half(shape, rank):
    return lax.broadcasted_iota(jnp.int32, shape, len(shape) - 1) < rank


def pair_columns(wide, vectors, rank):
    pairs = wide.reshape(-1, 2, vectors, 2 * rank)
    even, odd = pairs[:, 0], pairs[:, 1]
    return jnp.where(low_half(even.shape, rank), even, odd).astype(BF16)


def split_columns(paired, rank):
    count, vectors, lanes = paired.shape
    low = low_half((1, lanes), rank).astype(F32).astype(BF16)
    both = jnp.stack([paired * low, paired * (1 - low)], axis=1)
    return both.reshape(count * 2 * vectors, lanes)


def up_kernel(levels, rank, samples, basis, transfer, *outs):
    patch, _, vectors, sources = samples.shape
    basis2 = twice(basis[...])

    def project(i, carry):
        rows = samples[i].reshape(patch * vectors, sources)
        outs[0][i] = pair_columns(dot(rows, basis2, NT), vectors, rank)
        return carry

    lax.fori_loop(0, patch, project, 0)
    for level in range(levels):
        child = outs[level]
        matrix = twice(transfer[level])
        for row in range(child.shape[0] // 2):
            grouped = jnp.concatenate([child[2 * row], child[2 * row + 1]], axis=-1)
            wide = dot(grouped.reshape(-1, 4 * rank), matrix, NT)
            if level < levels - 1:
                outs[level + 1][row] = pair_columns(wide, vectors, rank)
            else:
                odd = lax.axis_index("gy") % 2
                lane = lax.broadcasted_iota(jnp.int32, wide.shape, 1)
                own = (lane >= odd * rank) & (lane < (odd + 1) * rank)
                outs[level + 1][...] = jnp.where(own, wide, 0.0).astype(BF16)


def span(side, size, width):
    if side == 0:
        return pl.ds(0, size), pl.ds(width, size)
    if side > 0:
        return pl.ds(size - width, width), pl.ds(0, width)
    return pl.ds(0, width), pl.ds(width + size, width)


def main_kernel(levels, rank, steps, offsets, counts, *refs):
    samples = refs[0]
    coeffs = refs[1 : 1 + levels]
    (top, codes, codes_upper, basis, transfer, coupling, shifted, near, out) = refs[
        1 + levels : 10 + levels
    ]
    scratch = refs[10 + levels :]
    codes_flat, masks, tops, total_near, top_rim, bottom_rim, left_rim, right_rim = scratch[:8]
    send, recv, local, top_send, top_recv = scratch[8:13]
    padded = scratch[13 : 13 + levels]
    uppers = scratch[13 + levels : 13 + levels + steps]
    downs = scratch[13 + levels + steps :]
    patch, _, vectors, sources = out.shape
    across, along = counts
    total = across * along
    lanes = 2 * rank
    wide = 36 * rank
    row_index, col_index = lax.axis_index("gx"), lax.axis_index("gy")
    me = row_index * along + col_index

    for rim in (top_rim, bottom_rim, left_rim, right_rim):
        rim[...] = jnp.zeros(rim.shape, BF16)
    for level in range(levels):
        target = padded[level]
        rows, cols = target.shape[:2]
        for spot in (
            (pl.ds(0, 2), pl.ds(0, cols)),
            (pl.ds(rows - 2, 2), pl.ds(0, cols)),
            (pl.ds(2, rows - 4), pl.ds(0, 1)),
            (pl.ds(2, rows - 4), pl.ds(cols - 1, 1)),
        ):
            target[spot[0], spot[1]] = jnp.zeros(
                (spot[0].size, spot[1].size, vectors, lanes), BF16
            )

    def place(device):
        return (device // along, device % along)

    barrier = pltpu.get_barrier_semaphore()

    def greet(step, carry):
        pl.semaphore_signal(
            barrier, inc=1, device_id=place((me + step) % total), device_id_type=MESH
        )
        return carry

    lax.fori_loop(1, total, greet, 0)

    def top_copy(step, sender):
        return pltpu.make_async_remote_copy(
            src_ref=top,
            dst_ref=tops.at[sender // along, sender % along],
            send_sem=top_send.at[step],
            recv_sem=top_recv.at[step],
            device_id=place((me + step) % total),
            device_id_type=MESH,
        )

    def coeff_copy(level, number):
        sx, sy = SIDES[number]
        size_x, size_y = coeffs[level].shape[:2]
        rows_from, rows_to = span(sx, size_x, 2)
        cols_from, cols_to = span(sy, size_y, 1)
        return pltpu.make_async_remote_copy(
            src_ref=coeffs[level].at[rows_from, cols_from],
            dst_ref=padded[level].at[rows_to, cols_to],
            send_sem=send.at[level, number],
            recv_sem=recv.at[level, number],
            device_id=(row_index + sx, col_index + sy),
            device_id_type=MESH,
        )

    def sample_copy(number):
        sx, sy = SIDES[number]
        rows_from, _ = span(sx, patch, 1)
        cols_from, cols_to = span(sy, patch, 1)
        if sx == 0:
            rim = left_rim if sy > 0 else right_rim
            spot = rim.at[pl.ds(1, patch), pl.ds(0, 1)]
        else:
            rim = top_rim if sx > 0 else bottom_rim
            spot = rim.at[pl.ds(0, 1), cols_to]
        return pltpu.make_async_remote_copy(
            src_ref=samples.at[rows_from, cols_from],
            dst_ref=spot,
            send_sem=send.at[levels, number],
            recv_sem=recv.at[levels, number],
            device_id=(row_index + sx, col_index + sy),
            device_id_type=MESH,
        )

    def inside(sx, sy):
        there_row, there_col = row_index + sx, col_index + sy
        return (there_row >= 0) & (there_row < across) & (there_col >= 0) & (there_col < along)

    own = [
        pltpu.make_async_copy(
            coeffs[level],
            padded[level].at[
                pl.ds(2, coeffs[level].shape[0]), pl.ds(1, coeffs[level].shape[1])
            ],
            local.at[level],
        )
        for level in range(levels)
    ]
    own.append(
        pltpu.make_async_copy(top, tops.at[row_index, col_index], local.at[levels])
    )
    for copy in own:
        copy.start()

    for level in range(levels):
        size = patch >> level
        for row in range(size):
            begin = (row << level) * patch * levels + level
            codes_flat[offsets[level] + row * size : offsets[level] + (row + 1) * size, :] = codes[
                pl.ds(begin, size, stride=levels << level), :
            ]
    codes_flat[offsets[levels] : offsets[levels] + codes_upper.shape[0], :] = codes_upper[...]
    code_lane = lax.broadcasted_iota(jnp.int32, (128, wide), 1) // rank
    code_row = lax.broadcasted_iota(jnp.int32, (128, wide), 0)
    widen = (code_lane == code_row).astype(F32).astype(BF16)
    group = 64

    def member(number, carry):
        start = pl.multiple_of(number * group, group)
        listed = codes_flat[pl.ds(start, group), :]
        code = lax.broadcasted_iota(jnp.int32, (group, 128), 1)
        found = jnp.zeros((group, 128), F32)
        for slot in range(listed.shape[1]):
            found = jnp.where(listed[:, slot : slot + 1] == code, 1.0, found)
        masks[pl.ds(start, group), :] = dot(found.astype(BF16), widen, NN)
        return carry

    lax.fori_loop(0, masks.shape[0] // group, member, 0)

    pl.semaphore_wait(barrier, total - 1)

    def start_top(step, carry):
        top_copy(step, me).start()
        return carry

    lax.fori_loop(1, total, start_top, 0)
    for number, (sx, sy) in enumerate(SIDES):

        @pl.when(inside(sx, sy))
        def _():
            for level in range(levels):
                coeff_copy(level, number).start()

    for number, (sx, sy) in enumerate(SIDES):

        @pl.when(inside(sx, sy))
        def _():
            sample_copy(number).start()

    def near_row(row, row_steps):
        blank = jnp.zeros((1, vectors, sources), BF16)
        left = []
        for row_step in row_steps:
            line = samples[row + row_step - 1]
            left.append(jnp.concatenate([blank, line[: patch - 1]], axis=0))
            left.append(line)
            left.append(jnp.concatenate([line[1:], blank], axis=0))
        left = jnp.concatenate([part.reshape(-1, sources) for part in left], axis=-1)
        flat = jnp.concatenate(
            [near[3 * row_step + step] for row_step in row_steps for step in range(3)], axis=-1
        )
        total_near[row] = dot(left, flat, NT)

    near_row(0, (1, 2))
    near_row(patch - 1, (0, 1))

    def near_body(row, carry):
        near_row(row, (0, 1, 2))
        return carry

    lax.fori_loop(1, patch - 1, near_body, 0)

    for copy in own:
        copy.wait()
    for number, (sx, sy) in enumerate(SIDES):

        @pl.when(inside(-sx, -sy))
        def _():
            for level in range(levels):
                coeff_copy(level, number).wait_recv()

    def wait_top(step, carry):
        top_copy(step, (me + total - step) % total).wait_recv()
        return carry

    lax.fori_loop(1, total, wait_top, 0)

    def weights(level, row_bit, col_bit):
        source = coupling if col_bit else shifted
        flat = jnp.concatenate(
            [source[level, code + 1 - row_bit, :, 0 : 6 * rank] for code in range(6)], axis=-1
        )
        return twice(flat)

    def window(ref, row, col):
        return jnp.concatenate(
            [ref[row + code, col + step] for code in range(6) for step in range(3)], axis=-1
        )

    def masked(slab, mask_row):
        mask = jnp.broadcast_to(masks[pl.ds(mask_row, 1), :], (16, wide)).astype(BF16)
        return (slab.reshape(-1, 16, wide) * mask[None]).reshape(slab.shape)

    uppers[0][...] = jnp.zeros(uppers[0].shape, BF16)
    for row in range(across):
        for col in range(along // 2):
            uppers[0][row + 2, col + 1] = tops[row, 2 * col] + tops[row, 2 * col + 1]
    top_matrix = twice(transfer[levels])
    for step in range(steps - 1):
        child, parent = uppers[step], uppers[step + 1]
        parent[...] = jnp.zeros(parent.shape, BF16)
        rows, cols = across >> step, along >> (step + 1)
        for row in range(rows // 2):
            grouped = jnp.concatenate(
                [child[2 * row + 2, 1 : 1 + cols], child[2 * row + 3, 1 : 1 + cols]], axis=-1
            )
            lifted = dot(grouped.reshape(-1, 4 * rank), top_matrix, NT)
            parent[row + 2, 1 : 1 + cols // 2] = pair_columns(lifted, vectors, rank)
    low = low_half((vectors, lanes), rank)
    low_mask = low_half((1, lanes), rank).astype(F32).astype(BF16)
    images = []
    begin = offsets[levels]
    for step in range(steps):
        rows, cols = across >> step, along >> step
        row, col = row_index // 2**step, col_index // 2**step
        slab = window(uppers[step], 2 * (row // 2), col // 2)
        slab = masked(slab, begin + row * cols + col)
        bit = row % 2
        image = []
        for source in (shifted, coupling):
            flat = jnp.concatenate(
                [source[levels, code + 1 - bit, :, 0 : 6 * rank] for code in range(6)], axis=-1
            )
            image.append(dot(slab, twice(flat), NT))
        images.append(jnp.where(col % 2 == 0, image[0], image[1]))
        begin += rows * cols
    down = images[-1]
    for step in range(steps - 2, -1, -1):
        row, col = row_index // 2**step, col_index // 2**step
        carried = dot(down.astype(BF16) * low_mask, top_matrix, NN)
        part = jnp.where(row % 2 == 0, carried[:, :lanes], carried[:, lanes:])
        turned = pltpu.roll(part, rank, 1)
        part = jnp.where(low == (col % 2 == 0), part, turned)
        down = images[step] + part
    spread_top = down.astype(BF16) * low_mask

    def level_row(level, row):
        size = patch >> level
        if level == levels - 1:
            parent = spread_top
        else:
            parent = split_columns(downs[level + 1][row], rank)
        carried = dot(parent, twice(transfer[level]), NN)
        slabs = [window(padded[level], 2 * row, col) for col in range(size // 2)]
        for row_bit in range(2):
            image = []
            for col_bit in range(2):
                start = offsets[level] + (2 * row + row_bit) * size + col_bit
                left = jnp.concatenate(
                    [masked(slabs[col], start + 2 * col) for col in range(size // 2)], axis=0
                )
                image.append(dot(left, weights(level, row_bit, col_bit), NT))
            total = jnp.where(low_half(image[0].shape, rank), image[0], image[1])
            total = total + carried[:, row_bit * lanes : (row_bit + 1) * lanes]
            downs[level][2 * row + row_bit] = total.astype(BF16).reshape(-1, vectors, lanes)

    for level in range(levels - 1, -1, -1):
        count = patch >> (level + 1)
        if count <= 2:
            for row in range(count):
                level_row(level, row)
        else:

            def body(row, carry, level=level):
                level_row(level, row)
                return carry

            lax.fori_loop(0, count, body, 0)

    for number, (sx, sy) in enumerate(SIDES):

        @pl.when(inside(-sx, -sy))
        def _():
            sample_copy(number).wait_recv()

    for rim, column, step in ((left_rim, 0, 0), (right_rim, patch - 1, 2)):
        left = jnp.concatenate(
            [rim[part : part + patch, 0].reshape(-1, sources) for part in range(3)], axis=-1
        )
        flat = jnp.concatenate([near[3 * part + step] for part in range(3)], axis=-1)
        extra = dot(left, flat, NT).reshape(patch, vectors, sources)
        spot = pl.ds(column * vectors, vectors)
        total_near[:, spot, :] = total_near[:, spot, :] + extra
    for rim, row, step in ((top_rim, 0, 0), (bottom_rim, patch - 1, 6)):
        left = jnp.concatenate(
            [rim[0, part : part + patch].reshape(-1, sources) for part in range(3)], axis=-1
        )
        flat = jnp.concatenate([near[step + part] for part in range(3)], axis=-1)
        total_near[row] = total_near[row] + dot(left, flat, NT)
    basis2 = twice(basis[...])

    def finish(row, carry):
        summed = total_near[row] + dot(split_columns(downs[0][row], rank), basis2, NN)
        out[row] = summed.astype(BF16).reshape(patch, vectors, sources)
        return carry

    lax.fori_loop(0, patch, finish, 0)

    for number, (sx, sy) in enumerate(SIDES):

        @pl.when(inside(sx, sy))
        def _():
            for level in range(levels):
                coeff_copy(level, number).wait_send()
            sample_copy(number).wait_send()

    def sent_top(step, carry):
        top_copy(step, me).wait_send()
        return carry

    lax.fori_loop(1, total, sent_top, 0)


def shards(
    samples,
    leaf_basis,
    transfer,
    coupling,
    near_tiles,
    codes_local,
    counts_local,
    codes_upper,
    counts_upper,
):
    patch, _, vectors, sources = samples.shape
    rank = leaf_basis.shape[0]
    levels = transfer.shape[0] - 1
    lanes = 2 * rank
    across, along = lax.axis_size("gx"), lax.axis_size("gy")
    steps = 1
    while across >> steps >= 2:
        steps += 1
    vmem = pl.BlockSpec(memory_space=pltpu.VMEM)

    slot = jnp.arange(codes_local.shape[-1], dtype=jnp.int32)
    listed = jnp.where(slot < counts_local[..., None], codes_local, -1)
    listed = listed.reshape(-1, codes_local.shape[-1])
    listed_upper = jnp.where(slot < counts_upper[..., None], codes_upper, -1)

    shapes = [
        jax.ShapeDtypeStruct((patch >> level, patch >> (level + 1), vectors, lanes), BF16)
        for level in range(levels)
    ]
    shapes.append(jax.ShapeDtypeStruct((vectors, lanes), BF16))
    coeffs = pl.pallas_call(
        functools.partial(up_kernel, levels, rank),
        out_shape=shapes,
        in_specs=[vmem] * 3,
        out_specs=[vmem] * len(shapes),
        compiler_params=pltpu.CompilerParams(vmem_limit_bytes=VMEM_LIMIT),
        name="up",
    )(samples, leaf_basis, transfer)

    offsets = [0]
    for level in range(levels):
        offsets.append(offsets[-1] + (patch >> level) ** 2)
    rows = offsets[-1] + codes_upper.shape[0]
    rows = (rows + 63) // 64 * 64
    shifted = coupling[..., rank:]
    return pl.pallas_call(
        functools.partial(main_kernel, levels, rank, steps, offsets, (across, along)),
        out_shape=jax.ShapeDtypeStruct(samples.shape, BF16),
        in_specs=[vmem] * (levels + 10 - 1),
        out_specs=vmem,
        scratch_shapes=[
            pltpu.VMEM((rows, codes_local.shape[-1]), jnp.int32),
            pltpu.VMEM((rows, 36 * rank), F32),
            pltpu.VMEM((across, along, vectors, lanes), BF16),
            pltpu.VMEM((patch, patch * vectors, sources), F32),
            pltpu.VMEM((1, patch + 2, vectors, sources), BF16),
            pltpu.VMEM((1, patch + 2, vectors, sources), BF16),
            pltpu.VMEM((patch + 2, 1, vectors, sources), BF16),
            pltpu.VMEM((patch + 2, 1, vectors, sources), BF16),
            pltpu.SemaphoreType.DMA((levels + 1, len(SIDES))),
            pltpu.SemaphoreType.DMA((levels + 1, len(SIDES))),
            pltpu.SemaphoreType.DMA((levels + 1,)),
            pltpu.SemaphoreType.DMA((across * along,)),
            pltpu.SemaphoreType.DMA((across * along,)),
        ]
        + [
            pltpu.VMEM((shape.shape[0] + 4, shape.shape[1] + 2, vectors, lanes), BF16)
            for shape in shapes[:levels]
        ]
        + [
            pltpu.VMEM(((across >> step) + 4, (along >> (step + 1)) + 2, vectors, lanes), BF16)
            for step in range(steps)
        ]
        + [pltpu.VMEM(shape.shape, BF16) for shape in shapes[:levels]],
        compiler_params=pltpu.CompilerParams(
            collective_id=0, has_side_effects=True, vmem_limit_bytes=VMEM_LIMIT
        ),
        name="finish",
    )(samples, *coeffs, listed, listed_upper, leaf_basis, transfer, coupling, shifted, near_tiles)


def solution(mesh):
    placed = (
        P("gx", "gy", None, None),
        P(),
        P(),
        P(),
        P(),
        P("gx", "gy", None, None),
        P("gx", "gy", None),
        P(),
        P(),
    )
    return jax.shard_map(
        shards, mesh=mesh, in_specs=placed, out_specs=P("gx", "gy", None, None), check_vma=False
    )
```

```python
import functools

import jax
import jax.numpy as jnp
from jax import lax
from jax.experimental import pallas as pl
from jax.experimental.pallas import tpu as pltpu
from jax.sharding import PartitionSpec as P

MESH = pl.DeviceIdType.MESH
F32 = jnp.float32
BF16 = jnp.bfloat16
NT = (((1,), (1,)), ((), ()))
NN = (((1,), (0,)), ((), ()))
VMEM_LIMIT = 60 * 1024 * 1024
AXES = ("gx", "gy")
SIDES = [(sx, sy) for sx in (-1, 0, 1) for sy in (-1, 0, 1) if (sx, sy) != (0, 0)]


def dot(a, b, dims):
    return lax.dot_general(a, b, dims, preferred_element_type=F32)


def twice(matrix):
    return jnp.concatenate([matrix, matrix], axis=0)


def low_half(shape, rank):
    return lax.broadcasted_iota(jnp.int32, shape, len(shape) - 1) < rank


def pair_columns(wide, vectors, rank):
    pairs = wide.reshape(-1, 2, vectors, 2 * rank)
    even, odd = pairs[:, 0], pairs[:, 1]
    return jnp.where(low_half(even.shape, rank), even, odd).astype(BF16)


def split_columns(paired, rank):
    count, vectors, lanes = paired.shape
    low = low_half((1, lanes), rank).astype(F32).astype(BF16)
    both = jnp.stack([paired * low, paired * (1 - low)], axis=1)
    return both.reshape(count * 2 * vectors, lanes)


def span(side, size, width):
    if side == 0:
        return pl.ds(0, size), pl.ds(width, size)
    if side > 0:
        return pl.ds(size - width, width), pl.ds(0, width)
    return pl.ds(0, width), pl.ds(width + size, width)


def main_kernel(levels, rank, steps, offsets, counts, *refs):
    (samples, codes, listed_counts, codes_upper, counts_upper) = refs[:5]
    (basis, transfer, coupling, near, out) = refs[5:10]
    scratch = refs[10:]
    codes_flat, masks, tops, total_near, top_rim, bottom_rim, left_rim, right_rim = scratch[:8]
    send, recv, shifted, top_send, top_recv = scratch[8:13]
    padded = scratch[13 : 13 + levels]
    uppers = scratch[13 + levels : 13 + levels + steps]
    downs = scratch[13 + levels + steps :]
    patch, _, vectors, sources = out.shape
    across, along = counts
    total = across * along
    lanes = 2 * rank
    wide = 36 * rank
    row_index, col_index = lax.axis_index("gx"), lax.axis_index("gy")
    me = row_index * along + col_index

    for rim in (top_rim, bottom_rim, left_rim, right_rim):
        rim[...] = jnp.zeros(rim.shape, BF16)
    for level in range(levels):
        target = padded[level]
        rows, cols = target.shape[:2]
        for spot in (
            (pl.ds(0, 2), pl.ds(0, cols)),
            (pl.ds(rows - 2, 2), pl.ds(0, cols)),
            (pl.ds(2, rows - 4), pl.ds(0, 1)),
            (pl.ds(2, rows - 4), pl.ds(cols - 1, 1)),
        ):
            target[spot[0], spot[1]] = jnp.zeros(
                (spot[0].size, spot[1].size, vectors, lanes), BF16
            )

    def place(device):
        return (device // along, device % along)

    barrier = pltpu.get_barrier_semaphore()

    def greet(step, carry):
        pl.semaphore_signal(
            barrier, inc=1, device_id=place((me + step) % total), device_id_type=MESH
        )
        return carry

    lax.fori_loop(1, total, greet, 0)

    def top_copy(step, sender):
        return pltpu.make_async_remote_copy(
            src_ref=tops.at[row_index, col_index],
            dst_ref=tops.at[sender // along, sender % along],
            send_sem=top_send.at[step],
            recv_sem=top_recv.at[step],
            device_id=place((me + step) % total),
            device_id_type=MESH,
        )

    def coeff_copy(level, number):
        sx, sy = SIDES[number]
        rows_from, rows_to = span(sx, patch >> level, 2)
        cols_from, cols_to = span(sy, patch >> (level + 1), 1)
        rows_from = pl.ds(rows_from.start + 2, rows_from.size)
        cols_from = pl.ds(cols_from.start + 1, cols_from.size)
        return pltpu.make_async_remote_copy(
            src_ref=padded[level].at[rows_from, cols_from],
            dst_ref=padded[level].at[rows_to, cols_to],
            send_sem=send.at[level, number],
            recv_sem=recv.at[level, number],
            device_id=(row_index + sx, col_index + sy),
            device_id_type=MESH,
        )

    half = patch // 2

    def sample_copy(number, late=False):
        sx, sy = SIDES[number]
        rows_from, _ = span(sx, patch, 1)
        cols_from, cols_to = span(sy, patch, 1)
        if sx == 0:
            rim = left_rim if sy > 0 else right_rim
            rows_from = pl.ds(half if late else 0, half)
            spot = rim.at[pl.ds(1 + rows_from.start, half), pl.ds(0, 1)]
        else:
            rim = top_rim if sx > 0 else bottom_rim
            spot = rim.at[pl.ds(0, 1), cols_to]
        return pltpu.make_async_remote_copy(
            src_ref=samples.at[rows_from, cols_from],
            dst_ref=spot,
            send_sem=send.at[levels + late, number],
            recv_sem=recv.at[levels + late, number],
            device_id=(row_index + sx, col_index + sy),
            device_id_type=MESH,
        )

    def inside(sx, sy):
        there_row, there_col = row_index + sx, col_index + sy
        return (there_row >= 0) & (there_row < across) & (there_col >= 0) & (there_col < along)

    slots = codes.shape[-1]
    for level in range(levels):
        size = patch >> level
        for row in range(size):
            begin = (row << level) * patch * levels + level
            listed = codes[pl.ds(begin, size, stride=levels << level), :]
            count = listed_counts[row << level, pl.ds(0, size, stride=1 << level), :]
            used = lax.broadcasted_iota(jnp.int32, (size, slots), 1) < count[:, level : level + 1]
            spot = offsets[level] + row * size
            codes_flat[spot : spot + size, :] = jnp.where(used, listed, -1)
    begin = 0
    for step in range(steps):
        cols = along >> step
        index = begin + (row_index // 2**step) * cols + col_index // 2**step
        used = lax.broadcasted_iota(jnp.int32, (1, slots), 1) < counts_upper[index]
        spot = offsets[levels] + step
        codes_flat[spot : spot + 1, :] = jnp.where(used, codes_upper[pl.ds(index, 1), :], -1)
        begin += (across >> step) * cols
    code_lane = lax.broadcasted_iota(jnp.int32, (128, wide), 1) // rank
    code_row = lax.broadcasted_iota(jnp.int32, (128, wide), 0)
    widen = (code_lane == code_row).astype(F32).astype(BF16)
    group = 64

    def member(number, carry):
        start = pl.multiple_of(number * group, group)
        listed = codes_flat[pl.ds(start, group), :]
        code = lax.broadcasted_iota(jnp.int32, (group, 128), 1)
        found = jnp.zeros((group, 128), F32)
        for slot in range(listed.shape[1]):
            found = jnp.where(listed[:, slot : slot + 1] == code, 1.0, found)
        masks[pl.ds(start, group), :] = dot(found.astype(BF16), widen, NN)
        return carry

    lax.fori_loop(0, masks.shape[0] // group, member, 0)

    pl.semaphore_wait(barrier, total - 1)

    def start_top(step, carry):
        top_copy(step, me).start()
        return carry

    for number, (sx, sy) in enumerate(SIDES):

        @pl.when(inside(sx, sy))
        def _():
            sample_copy(number).start()

    own_basis = twice(basis[...])

    def project(i, carry):
        rows = samples[i].reshape(patch * vectors, sources)
        padded[0][i + 2, 1 : 1 + patch // 2] = pair_columns(
            dot(rows, own_basis, NT), vectors, rank
        )
        return carry

    lax.fori_loop(0, patch, project, 0)
    for level in range(levels):
        child = padded[level]
        matrix = twice(transfer[level])
        cols = patch >> (level + 1)
        for row in range(cols):
            grouped = jnp.concatenate(
                [child[2 * row + 2, 1 : 1 + cols], child[2 * row + 3, 1 : 1 + cols]], axis=-1
            )
            lifted = dot(grouped.reshape(-1, 4 * rank), matrix, NT)
            if level < levels - 1:
                padded[level + 1][row + 2, 1 : 1 + cols // 2] = pair_columns(
                    lifted, vectors, rank
                )
            else:
                odd = col_index % 2
                lane = lax.broadcasted_iota(jnp.int32, lifted.shape, 1)
                own = (lane >= odd * rank) & (lane < (odd + 1) * rank)
                tops[row_index, col_index] = jnp.where(own, lifted, 0.0).astype(BF16)

    for number, (sx, sy) in enumerate(SIDES):

        @pl.when(inside(sx, sy))
        def _():
            for level in range(levels):
                coeff_copy(level, number).start()

    lax.fori_loop(1, total, start_top, 0)
    for number, (sx, sy) in enumerate(SIDES):
        if sx == 0:

            @pl.when(inside(sx, sy))
            def _():
                sample_copy(number, True).start()

    def shift(number, carry):
        level, part = number // coupling.shape[1], number % coupling.shape[1]
        shifted[level, part] = coupling[level, part][:, rank:]
        return carry

    lax.fori_loop(0, coupling.shape[0] * coupling.shape[1], shift, 0)

    def near_row(row, row_steps):
        blank = jnp.zeros((1, vectors, sources), BF16)
        left = []
        for row_step in row_steps:
            line = samples[row + row_step - 1]
            left.append(jnp.concatenate([blank, line[: patch - 1]], axis=0))
            left.append(line)
            left.append(jnp.concatenate([line[1:], blank], axis=0))
        left = jnp.concatenate([part.reshape(-1, sources) for part in left], axis=-1)
        flat = jnp.concatenate(
            [near[3 * row_step + step] for row_step in row_steps for step in range(3)], axis=-1
        )
        total_near[row] = dot(left, flat, NT)

    near_row(0, (1, 2))
    near_row(patch - 1, (0, 1))

    def near_body(row, carry):
        near_row(row, (0, 1, 2))
        return carry

    lax.fori_loop(1, patch - 1, near_body, 0)

    for number, (sx, sy) in enumerate(SIDES):

        @pl.when(inside(-sx, -sy))
        def _():
            for level in range(levels):
                coeff_copy(level, number).wait_recv()

    def wait_top(step, carry):
        top_copy(step, (me + total - step) % total).wait_recv()
        return carry

    lax.fori_loop(1, total, wait_top, 0)

    def weights(level, row_bit, col_bit):
        source = coupling if col_bit else shifted
        flat = jnp.concatenate(
            [source[level, code + 1 - row_bit, :, 0 : 6 * rank] for code in range(6)], axis=-1
        )
        return twice(flat)

    def window(ref, row, col):
        return jnp.concatenate(
            [ref[row + code, col + step] for code in range(6) for step in range(3)], axis=-1
        )

    def masked(slab, mask_row):
        mask = jnp.broadcast_to(masks[pl.ds(mask_row, 1), :], (16, wide)).astype(BF16)
        return (slab.reshape(-1, 16, wide) * mask[None]).reshape(slab.shape)

    uppers[0][...] = jnp.zeros(uppers[0].shape, BF16)
    for row in range(across):
        for col in range(along // 2):
            uppers[0][row + 2, col + 1] = tops[row, 2 * col] + tops[row, 2 * col + 1]
    top_matrix = twice(transfer[levels])
    for step in range(steps - 1):
        child, parent = uppers[step], uppers[step + 1]
        parent[...] = jnp.zeros(parent.shape, BF16)
        rows, cols = across >> step, along >> (step + 1)
        for row in range(rows // 2):
            grouped = jnp.concatenate(
                [child[2 * row + 2, 1 : 1 + cols], child[2 * row + 3, 1 : 1 + cols]], axis=-1
            )
            lifted = dot(grouped.reshape(-1, 4 * rank), top_matrix, NT)
            parent[row + 2, 1 : 1 + cols // 2] = pair_columns(lifted, vectors, rank)
    low = low_half((vectors, lanes), rank)
    low_mask = low_half((1, lanes), rank).astype(F32).astype(BF16)
    images = []
    begin = offsets[levels]
    for step in range(steps):
        row, col = row_index // 2**step, col_index // 2**step
        slab = window(uppers[step], 2 * (row // 2), col // 2)
        slab = masked(slab, begin + step)
        bit = row % 2
        image = []
        for source in (shifted, coupling):
            flat = jnp.concatenate(
                [source[levels, code + 1 - bit, :, 0 : 6 * rank] for code in range(6)], axis=-1
            )
            image.append(dot(slab, twice(flat), NT))
        images.append(jnp.where(col % 2 == 0, image[0], image[1]))
    down = images[-1]
    for step in range(steps - 2, -1, -1):
        row, col = row_index // 2**step, col_index // 2**step
        carried = dot(down.astype(BF16) * low_mask, top_matrix, NN)
        part = jnp.where(row % 2 == 0, carried[:, :lanes], carried[:, lanes:])
        turned = pltpu.roll(part, rank, 1)
        part = jnp.where(low == (col % 2 == 0), part, turned)
        down = images[step] + part
    spread_top = down.astype(BF16) * low_mask

    def level_row(level, row):
        size = patch >> level
        if level == levels - 1:
            parent = spread_top
        else:
            parent = split_columns(downs[level + 1][row], rank)
        carried = dot(parent, twice(transfer[level]), NN)
        slabs = [window(padded[level], 2 * row, col) for col in range(size // 2)]
        for row_bit in range(2):
            image = []
            for col_bit in range(2):
                start = offsets[level] + (2 * row + row_bit) * size + col_bit
                left = jnp.concatenate(
                    [masked(slabs[col], start + 2 * col) for col in range(size // 2)], axis=0
                )
                image.append(dot(left, weights(level, row_bit, col_bit), NT))
            total = jnp.where(low_half(image[0].shape, rank), image[0], image[1])
            total = total + carried[:, row_bit * lanes : (row_bit + 1) * lanes]
            downs[level][2 * row + row_bit] = total.astype(BF16).reshape(-1, vectors, lanes)

    for level in range(levels - 1, -1, -1):
        count = patch >> (level + 1)
        if count <= 2:
            for row in range(count):
                level_row(level, row)
        else:

            def body(row, carry, level=level):
                level_row(level, row)
                return carry

            lax.fori_loop(0, count, body, 0)

    for number, (sx, sy) in enumerate(SIDES):

        @pl.when(inside(-sx, -sy))
        def _():
            sample_copy(number).wait_recv()
            if sx == 0:
                sample_copy(number, True).wait_recv()

    for rim, column, step in ((left_rim, 0, 0), (right_rim, patch - 1, 2)):
        left = jnp.concatenate(
            [rim[part : part + patch, 0].reshape(-1, sources) for part in range(3)], axis=-1
        )
        flat = jnp.concatenate([near[3 * part + step] for part in range(3)], axis=-1)
        extra = dot(left, flat, NT).reshape(patch, vectors, sources)
        spot = pl.ds(column * vectors, vectors)
        total_near[:, spot, :] = total_near[:, spot, :] + extra
    for rim, row, step in ((top_rim, 0, 0), (bottom_rim, patch - 1, 6)):
        left = jnp.concatenate(
            [rim[0, part : part + patch].reshape(-1, sources) for part in range(3)], axis=-1
        )
        flat = jnp.concatenate([near[step + part] for part in range(3)], axis=-1)
        total_near[row] = total_near[row] + dot(left, flat, NT)
    basis2 = twice(basis[...])

    def finish(row, carry):
        summed = total_near[row] + dot(split_columns(downs[0][row], rank), basis2, NN)
        out[row] = summed.astype(BF16).reshape(patch, vectors, sources)
        return carry

    lax.fori_loop(0, patch, finish, 0)

    for number, (sx, sy) in enumerate(SIDES):

        @pl.when(inside(sx, sy))
        def _():
            for level in range(levels):
                coeff_copy(level, number).wait_send()
            sample_copy(number).wait_send()
            if sx == 0:
                sample_copy(number, True).wait_send()

    def sent_top(step, carry):
        top_copy(step, me).wait_send()
        return carry

    lax.fori_loop(1, total, sent_top, 0)


def shards(
    samples,
    leaf_basis,
    transfer,
    coupling,
    near_tiles,
    codes_local,
    counts_local,
    codes_upper,
    counts_upper,
):
    patch, _, vectors, sources = samples.shape
    rank = leaf_basis.shape[0]
    levels = transfer.shape[0] - 1
    lanes = 2 * rank
    across, along = lax.axis_size("gx"), lax.axis_size("gy")
    steps = 1
    while across >> steps >= 2:
        steps += 1
    vmem = pl.BlockSpec(memory_space=pltpu.VMEM)

    shapes = [
        jax.ShapeDtypeStruct((patch >> level, patch >> (level + 1), vectors, lanes), BF16)
        for level in range(levels)
    ]
    offsets = [0]
    for level in range(levels):
        offsets.append(offsets[-1] + (patch >> level) ** 2)
    rows = offsets[-1] + steps
    rows = (rows + 63) // 64 * 64
    return pl.pallas_call(
        functools.partial(main_kernel, levels, rank, steps, offsets, (across, along)),
        out_shape=jax.ShapeDtypeStruct(samples.shape, BF16),
        in_specs=[vmem] * 4 + [pl.BlockSpec(memory_space=pltpu.SMEM)] + [vmem] * 4,
        out_specs=vmem,
        scratch_shapes=[
            pltpu.VMEM((rows, codes_local.shape[-1]), jnp.int32),
            pltpu.VMEM((rows, 36 * rank), F32),
            pltpu.VMEM((across, along, vectors, lanes), BF16),
            pltpu.VMEM((patch, patch * vectors, sources), F32),
            pltpu.VMEM((1, patch + 2, vectors, sources), BF16),
            pltpu.VMEM((1, patch + 2, vectors, sources), BF16),
            pltpu.VMEM((patch + 2, 1, vectors, sources), BF16),
            pltpu.VMEM((patch + 2, 1, vectors, sources), BF16),
            pltpu.SemaphoreType.DMA((levels + 2, len(SIDES))),
            pltpu.SemaphoreType.DMA((levels + 2, len(SIDES))),
            pltpu.VMEM(coupling.shape[:3] + (6 * rank,), BF16),
            pltpu.SemaphoreType.DMA((across * along,)),
            pltpu.SemaphoreType.DMA((across * along,)),
        ]
        + [
            pltpu.VMEM((shape.shape[0] + 4, shape.shape[1] + 2, vectors, lanes), BF16)
            for shape in shapes[:levels]
        ]
        + [
            pltpu.VMEM(((across >> step) + 4, (along >> (step + 1)) + 2, vectors, lanes), BF16)
            for step in range(steps)
        ]
        + [pltpu.VMEM(shape.shape, BF16) for shape in shapes[:levels]],
        compiler_params=pltpu.CompilerParams(
            collective_id=0, has_side_effects=True, vmem_limit_bytes=VMEM_LIMIT
        ),
        name="finish",
    )(
        samples,
        codes_local.reshape(-1, codes_local.shape[-1]),
        counts_local,
        codes_upper,
        counts_upper,
        leaf_basis,
        transfer,
        coupling,
        near_tiles,
    )


def solution(mesh):
    placed = (
        P("gx", "gy", None, None),
        P(),
        P(),
        P(),
        P(),
        P("gx", "gy", None, None),
        P("gx", "gy", None),
        P(),
        P(),
    )
    return jax.shard_map(
        shards, mesh=mesh, in_specs=placed, out_specs=P("gx", "gy", None, None), check_vma=False
    )
```

```python
import functools

import jax
import jax.numpy as jnp
from jax import lax
from jax.experimental import pallas as pl
from jax.experimental.pallas import tpu as pltpu
from jax.sharding import PartitionSpec as P

MESH = pl.DeviceIdType.MESH
F32 = jnp.float32
BF16 = jnp.bfloat16
NT = (((1,), (1,)), ((), ()))
NN = (((1,), (0,)), ((), ()))
VMEM_LIMIT = 60 * 1024 * 1024
AXES = ("gx", "gy")
SIDES = [(sx, sy) for sx in (-1, 0, 1) for sy in (-1, 0, 1) if (sx, sy) != (0, 0)]


def dot(a, b, dims):
    return lax.dot_general(a, b, dims, preferred_element_type=F32)


def twice(matrix):
    return jnp.concatenate([matrix, matrix], axis=0)


def low_half(shape, rank):
    return lax.broadcasted_iota(jnp.int32, shape, len(shape) - 1) < rank


def pair_columns(wide, vectors, rank):
    pairs = wide.reshape(-1, 2, vectors, 2 * rank)
    even, odd = pairs[:, 0], pairs[:, 1]
    return jnp.where(low_half(even.shape, rank), even, odd).astype(BF16)


def split_columns(paired, rank):
    count, vectors, lanes = paired.shape
    low = low_half((1, lanes), rank).astype(F32).astype(BF16)
    both = jnp.stack([paired * low, paired * (1 - low)], axis=1)
    return both.reshape(count * 2 * vectors, lanes)


def span(side, size, width):
    if side == 0:
        return pl.ds(0, size), pl.ds(width, size)
    if side > 0:
        return pl.ds(size - width, width), pl.ds(0, width)
    return pl.ds(0, width), pl.ds(width + size, width)


def main_kernel(levels, rank, steps, offsets, counts, *refs):
    (samples, codes, listed_counts, codes_upper, counts_upper) = refs[:5]
    (basis, transfer, coupling, near, near_out, leaf_down) = refs[5:11]
    scratch = refs[11:]
    codes_flat, masks, tops, total_near, top_rim, bottom_rim, left_rim, right_rim = scratch[:8]
    send, recv, shifted, top_send, top_recv = scratch[8:13]
    padded = scratch[13 : 13 + levels]
    uppers = scratch[13 + levels : 13 + levels + steps]
    downs = (leaf_down, *scratch[13 + levels + steps :])
    patch, _, vectors, sources = samples.shape
    across, along = counts
    total = across * along
    lanes = 2 * rank
    wide = 36 * rank
    row_index, col_index = lax.axis_index("gx"), lax.axis_index("gy")
    me = row_index * along + col_index

    for rim in (top_rim, bottom_rim, left_rim, right_rim):
        rim[...] = jnp.zeros(rim.shape, BF16)
    for level in range(levels):
        target = padded[level]
        rows, cols = target.shape[:2]
        for spot in (
            (pl.ds(0, 2), pl.ds(0, cols)),
            (pl.ds(rows - 2, 2), pl.ds(0, cols)),
            (pl.ds(2, rows - 4), pl.ds(0, 1)),
            (pl.ds(2, rows - 4), pl.ds(cols - 1, 1)),
        ):
            target[spot[0], spot[1]] = jnp.zeros(
                (spot[0].size, spot[1].size, vectors, lanes), BF16
            )

    def place(device):
        return (device // along, device % along)

    barrier = pltpu.get_barrier_semaphore()

    def greet(step, carry):
        pl.semaphore_signal(
            barrier, inc=1, device_id=place((me + step) % total), device_id_type=MESH
        )
        return carry

    lax.fori_loop(1, total, greet, 0)

    def top_copy(step, sender):
        return pltpu.make_async_remote_copy(
            src_ref=tops.at[row_index, col_index],
            dst_ref=tops.at[sender // along, sender % along],
            send_sem=top_send.at[step],
            recv_sem=top_recv.at[step],
            device_id=place((me + step) % total),
            device_id_type=MESH,
        )

    def coeff_copy(level, number):
        sx, sy = SIDES[number]
        rows_from, rows_to = span(sx, patch >> level, 2)
        cols_from, cols_to = span(sy, patch >> (level + 1), 1)
        rows_from = pl.ds(rows_from.start + 2, rows_from.size)
        cols_from = pl.ds(cols_from.start + 1, cols_from.size)
        return pltpu.make_async_remote_copy(
            src_ref=padded[level].at[rows_from, cols_from],
            dst_ref=padded[level].at[rows_to, cols_to],
            send_sem=send.at[level, number],
            recv_sem=recv.at[level, number],
            device_id=(row_index + sx, col_index + sy),
            device_id_type=MESH,
        )

    half = patch // 2

    def sample_copy(number, late=False):
        sx, sy = SIDES[number]
        rows_from, _ = span(sx, patch, 1)
        cols_from, cols_to = span(sy, patch, 1)
        if sx == 0:
            rim = left_rim if sy > 0 else right_rim
            rows_from = pl.ds(half if late else 0, half)
            spot = rim.at[pl.ds(1 + rows_from.start, half), pl.ds(0, 1)]
        else:
            rim = top_rim if sx > 0 else bottom_rim
            spot = rim.at[pl.ds(0, 1), cols_to]
        return pltpu.make_async_remote_copy(
            src_ref=samples.at[rows_from, cols_from],
            dst_ref=spot,
            send_sem=send.at[levels + late, number],
            recv_sem=recv.at[levels + late, number],
            device_id=(row_index + sx, col_index + sy),
            device_id_type=MESH,
        )

    def inside(sx, sy):
        there_row, there_col = row_index + sx, col_index + sy
        return (there_row >= 0) & (there_row < across) & (there_col >= 0) & (there_col < along)

    slots = codes.shape[-1]
    for level in range(levels):
        size = patch >> level
        for row in range(size):
            begin = (row << level) * patch * levels + level
            listed = codes[pl.ds(begin, size, stride=levels << level), :]
            count = listed_counts[row << level, pl.ds(0, size, stride=1 << level), :]
            used = lax.broadcasted_iota(jnp.int32, (size, slots), 1) < count[:, level : level + 1]
            spot = offsets[level] + row * size
            codes_flat[spot : spot + size, :] = jnp.where(used, listed, -1)
    begin = 0
    for step in range(steps):
        cols = along >> step
        index = begin + (row_index // 2**step) * cols + col_index // 2**step
        used = lax.broadcasted_iota(jnp.int32, (1, slots), 1) < counts_upper[index]
        spot = offsets[levels] + step
        codes_flat[spot : spot + 1, :] = jnp.where(used, codes_upper[pl.ds(index, 1), :], -1)
        begin += (across >> step) * cols
    code_lane = lax.broadcasted_iota(jnp.int32, (128, wide), 1) // rank
    code_row = lax.broadcasted_iota(jnp.int32, (128, wide), 0)
    widen = (code_lane == code_row).astype(F32).astype(BF16)
    group = 64

    def member(number, carry):
        start = pl.multiple_of(number * group, group)
        listed = codes_flat[pl.ds(start, group), :]
        code = lax.broadcasted_iota(jnp.int32, (group, 128), 1)
        found = jnp.zeros((group, 128), F32)
        for slot in range(listed.shape[1]):
            found = jnp.where(listed[:, slot : slot + 1] == code, 1.0, found)
        masks[pl.ds(start, group), :] = dot(found.astype(BF16), widen, NN)
        return carry

    lax.fori_loop(0, masks.shape[0] // group, member, 0)

    pl.semaphore_wait(barrier, total - 1)

    def start_top(step, carry):
        top_copy(step, me).start()
        return carry

    for number, (sx, sy) in enumerate(SIDES):

        @pl.when(inside(sx, sy))
        def _():
            sample_copy(number).start()

    own_basis = twice(basis[...])

    def project(i, carry):
        rows = samples[i].reshape(patch * vectors, sources)
        padded[0][i + 2, 1 : 1 + patch // 2] = pair_columns(
            dot(rows, own_basis, NT), vectors, rank
        )
        return carry

    lax.fori_loop(0, patch, project, 0)
    for level in range(levels):
        child = padded[level]
        matrix = twice(transfer[level])
        cols = patch >> (level + 1)
        for row in range(cols):
            grouped = jnp.concatenate(
                [child[2 * row + 2, 1 : 1 + cols], child[2 * row + 3, 1 : 1 + cols]], axis=-1
            )
            lifted = dot(grouped.reshape(-1, 4 * rank), matrix, NT)
            if level < levels - 1:
                padded[level + 1][row + 2, 1 : 1 + cols // 2] = pair_columns(
                    lifted, vectors, rank
                )
            else:
                odd = col_index % 2
                lane = lax.broadcasted_iota(jnp.int32, lifted.shape, 1)
                own = (lane >= odd * rank) & (lane < (odd + 1) * rank)
                tops[row_index, col_index] = jnp.where(own, lifted, 0.0).astype(BF16)

    for number, (sx, sy) in enumerate(SIDES):

        @pl.when(inside(sx, sy))
        def _():
            for level in range(levels):
                coeff_copy(level, number).start()

    lax.fori_loop(1, total, start_top, 0)
    for number, (sx, sy) in enumerate(SIDES):
        if sx == 0:

            @pl.when(inside(sx, sy))
            def _():
                sample_copy(number, True).start()

    def shift(number, carry):
        level, part = number // coupling.shape[1], number % coupling.shape[1]
        shifted[level, part] = coupling[level, part][:, rank:]
        return carry

    lax.fori_loop(0, coupling.shape[0] * coupling.shape[1], shift, 0)

    def near_row(row, row_steps):
        blank = jnp.zeros((1, vectors, sources), BF16)
        left = []
        for row_step in row_steps:
            line = samples[row + row_step - 1]
            left.append(jnp.concatenate([blank, line[: patch - 1]], axis=0))
            left.append(line)
            left.append(jnp.concatenate([line[1:], blank], axis=0))
        left = jnp.concatenate([part.reshape(-1, sources) for part in left], axis=-1)
        flat = jnp.concatenate(
            [near[3 * row_step + step] for row_step in row_steps for step in range(3)], axis=-1
        )
        total_near[row] = dot(left, flat, NT)

    near_row(0, (1, 2))
    near_row(patch - 1, (0, 1))

    def near_body(row, carry):
        near_row(row, (0, 1, 2))
        return carry

    lax.fori_loop(1, patch - 1, near_body, 0)

    for number, (sx, sy) in enumerate(SIDES):

        @pl.when(inside(-sx, -sy))
        def _():
            for level in range(levels):
                coeff_copy(level, number).wait_recv()

    def wait_top(step, carry):
        top_copy(step, (me + total - step) % total).wait_recv()
        return carry

    lax.fori_loop(1, total, wait_top, 0)

    def weights(level, row_bit, col_bit):
        source = coupling if col_bit else shifted
        flat = jnp.concatenate(
            [source[level, code + 1 - row_bit, :, 0 : 6 * rank] for code in range(6)], axis=-1
        )
        return twice(flat)

    def window(ref, row, col):
        return jnp.concatenate(
            [ref[row + code, col + step] for code in range(6) for step in range(3)], axis=-1
        )

    def masked(slab, mask_row):
        mask = jnp.broadcast_to(masks[pl.ds(mask_row, 1), :], (16, wide)).astype(BF16)
        return (slab.reshape(-1, 16, wide) * mask[None]).reshape(slab.shape)

    uppers[0][...] = jnp.zeros(uppers[0].shape, BF16)
    for row in range(across):
        for col in range(along // 2):
            uppers[0][row + 2, col + 1] = tops[row, 2 * col] + tops[row, 2 * col + 1]
    top_matrix = twice(transfer[levels])
    for step in range(steps - 1):
        child, parent = uppers[step], uppers[step + 1]
        parent[...] = jnp.zeros(parent.shape, BF16)
        rows, cols = across >> step, along >> (step + 1)
        for row in range(rows // 2):
            grouped = jnp.concatenate(
                [child[2 * row + 2, 1 : 1 + cols], child[2 * row + 3, 1 : 1 + cols]], axis=-1
            )
            lifted = dot(grouped.reshape(-1, 4 * rank), top_matrix, NT)
            parent[row + 2, 1 : 1 + cols // 2] = pair_columns(lifted, vectors, rank)
    low = low_half((vectors, lanes), rank)
    low_mask = low_half((1, lanes), rank).astype(F32).astype(BF16)
    images = []
    begin = offsets[levels]
    for step in range(steps):
        row, col = row_index // 2**step, col_index // 2**step
        slab = window(uppers[step], 2 * (row // 2), col // 2)
        slab = masked(slab, begin + step)
        bit = row % 2
        image = []
        for source in (shifted, coupling):
            flat = jnp.concatenate(
                [source[levels, code + 1 - bit, :, 0 : 6 * rank] for code in range(6)], axis=-1
            )
            image.append(dot(slab, twice(flat), NT))
        images.append(jnp.where(col % 2 == 0, image[0], image[1]))
    down = images[-1]
    for step in range(steps - 2, -1, -1):
        row, col = row_index // 2**step, col_index // 2**step
        carried = dot(down.astype(BF16) * low_mask, top_matrix, NN)
        part = jnp.where(row % 2 == 0, carried[:, :lanes], carried[:, lanes:])
        turned = pltpu.roll(part, rank, 1)
        part = jnp.where(low == (col % 2 == 0), part, turned)
        down = images[step] + part
    spread_top = down.astype(BF16) * low_mask

    def level_rows(level, rows):
        size = patch >> level
        if level == levels - 1:
            parent = spread_top
        else:
            parent = jnp.concatenate(
                [split_columns(downs[level + 1][row], rank) for row in rows], axis=0
            )
        carried = dot(parent, twice(transfer[level]), NN)
        slabs = [
            (row, col, window(padded[level], 2 * row, col))
            for row in rows
            for col in range(size // 2)
        ]
        for row_bit in range(2):
            image = []
            for col_bit in range(2):
                left = jnp.concatenate(
                    [
                        masked(
                            slab, offsets[level] + (2 * row + row_bit) * size + col_bit + 2 * col
                        )
                        for row, col, slab in slabs
                    ],
                    axis=0,
                )
                image.append(dot(left, weights(level, row_bit, col_bit), NT))
            summed = jnp.where(low_half(image[0].shape, rank), image[0], image[1])
            summed = summed + carried[:, row_bit * lanes : (row_bit + 1) * lanes]
            summed = summed.astype(BF16).reshape(len(rows), -1, vectors, lanes)
            for number, row in enumerate(rows):
                downs[level][2 * row + row_bit] = summed[number]

    for level in range(levels - 1, -1, -1):
        count = patch >> (level + 1)
        if count <= 2:
            level_rows(level, list(range(count)))
        else:

            def body(pair, carry, level=level):
                level_rows(level, [2 * pair, 2 * pair + 1])
                return carry

            lax.fori_loop(0, count // 2, body, 0)

    for number, (sx, sy) in enumerate(SIDES):

        @pl.when(inside(-sx, -sy))
        def _():
            sample_copy(number).wait_recv()
            if sx == 0:
                sample_copy(number, True).wait_recv()

    for rim, column, step in ((left_rim, 0, 0), (right_rim, patch - 1, 2)):
        left = jnp.concatenate(
            [rim[part : part + patch, 0].reshape(-1, sources) for part in range(3)], axis=-1
        )
        flat = jnp.concatenate([near[3 * part + step] for part in range(3)], axis=-1)
        extra = dot(left, flat, NT).reshape(patch, vectors, sources)
        spot = pl.ds(column * vectors, vectors)
        total_near[:, spot, :] = total_near[:, spot, :] + extra
    for rim, row, step in ((top_rim, 0, 0), (bottom_rim, patch - 1, 6)):
        left = jnp.concatenate(
            [rim[0, part : part + patch].reshape(-1, sources) for part in range(3)], axis=-1
        )
        flat = jnp.concatenate([near[step + part] for part in range(3)], axis=-1)
        total_near[row] = total_near[row] + dot(left, flat, NT)
    def round_row(row, carry):
        near_out[row] = total_near[row].astype(BF16)
        return carry

    lax.fori_loop(0, patch, round_row, 0)

    for number, (sx, sy) in enumerate(SIDES):

        @pl.when(inside(sx, sy))
        def _():
            for level in range(levels):
                coeff_copy(level, number).wait_send()
            sample_copy(number).wait_send()
            if sx == 0:
                sample_copy(number, True).wait_send()

    def sent_top(step, carry):
        top_copy(step, me).wait_send()
        return carry

    lax.fori_loop(1, total, sent_top, 0)


def finish_kernel(rank, near_sum, leaf_down, basis, out):
    rows, patch, vectors, sources = out.shape
    basis2 = twice(basis[...])
    for row in range(rows):
        summed = near_sum[row].astype(F32) + dot(split_columns(leaf_down[row], rank), basis2, NN)
        out[row] = summed.astype(BF16).reshape(patch, vectors, sources)


def shards(
    samples,
    leaf_basis,
    transfer,
    coupling,
    near_tiles,
    codes_local,
    counts_local,
    codes_upper,
    counts_upper,
):
    patch, _, vectors, sources = samples.shape
    rank = leaf_basis.shape[0]
    levels = transfer.shape[0] - 1
    lanes = 2 * rank
    across, along = lax.axis_size("gx"), lax.axis_size("gy")
    steps = 1
    while across >> steps >= 2:
        steps += 1
    vmem = pl.BlockSpec(memory_space=pltpu.VMEM)

    shapes = [
        jax.ShapeDtypeStruct((patch >> level, patch >> (level + 1), vectors, lanes), BF16)
        for level in range(levels)
    ]
    offsets = [0]
    for level in range(levels):
        offsets.append(offsets[-1] + (patch >> level) ** 2)
    rows = offsets[-1] + steps
    rows = (rows + 63) // 64 * 64
    near_sum, leaf_down = pl.pallas_call(
        functools.partial(main_kernel, levels, rank, steps, offsets, (across, along)),
        out_shape=[
            jax.ShapeDtypeStruct((patch, patch * vectors, sources), BF16),
            shapes[0],
        ],
        in_specs=[vmem] * 4 + [pl.BlockSpec(memory_space=pltpu.SMEM)] + [vmem] * 4,
        out_specs=[vmem, vmem],
        scratch_shapes=[
            pltpu.VMEM((rows, codes_local.shape[-1]), jnp.int32),
            pltpu.VMEM((rows, 36 * rank), F32),
            pltpu.VMEM((across, along, vectors, lanes), BF16),
            pltpu.VMEM((patch, patch * vectors, sources), F32),
            pltpu.VMEM((1, patch + 2, vectors, sources), BF16),
            pltpu.VMEM((1, patch + 2, vectors, sources), BF16),
            pltpu.VMEM((patch + 2, 1, vectors, sources), BF16),
            pltpu.VMEM((patch + 2, 1, vectors, sources), BF16),
            pltpu.SemaphoreType.DMA((levels + 2, len(SIDES))),
            pltpu.SemaphoreType.DMA((levels + 2, len(SIDES))),
            pltpu.VMEM(coupling.shape[:3] + (6 * rank,), BF16),
            pltpu.SemaphoreType.DMA((across * along,)),
            pltpu.SemaphoreType.DMA((across * along,)),
        ]
        + [
            pltpu.VMEM((shape.shape[0] + 4, shape.shape[1] + 2, vectors, lanes), BF16)
            for shape in shapes[:levels]
        ]
        + [
            pltpu.VMEM(((across >> step) + 4, (along >> (step + 1)) + 2, vectors, lanes), BF16)
            for step in range(steps)
        ]
        + [pltpu.VMEM(shape.shape, BF16) for shape in shapes[1:levels]],
        compiler_params=pltpu.CompilerParams(
            collective_id=0, has_side_effects=True, vmem_limit_bytes=VMEM_LIMIT
        ),
        name="main",
    )(
        samples,
        codes_local.reshape(-1, codes_local.shape[-1]),
        counts_local,
        codes_upper,
        counts_upper,
        leaf_basis,
        transfer,
        coupling,
        near_tiles,
    )
    strip = patch // 4
    return pl.pallas_call(
        functools.partial(finish_kernel, rank),
        out_shape=jax.ShapeDtypeStruct(samples.shape, BF16),
        grid=(patch // strip,),
        in_specs=[
            pl.BlockSpec((strip, patch * vectors, sources), lambda i: (i, 0, 0)),
            pl.BlockSpec((strip, patch // 2, vectors, lanes), lambda i: (i, 0, 0, 0)),
            pl.BlockSpec((rank, sources), lambda i: (0, 0)),
        ],
        out_specs=pl.BlockSpec((strip, patch, vectors, sources), lambda i: (i, 0, 0, 0)),
        name="finish",
    )(near_sum, leaf_down, leaf_basis)


def solution(mesh):
    placed = (
        P("gx", "gy", None, None),
        P(),
        P(),
        P(),
        P(),
        P("gx", "gy", None, None),
        P("gx", "gy", None),
        P(),
        P(),
    )
    return jax.shard_map(
        shards, mesh=mesh, in_specs=placed, out_specs=P("gx", "gy", None, None), check_vma=False
    )
```

```python
import functools

import jax
import jax.numpy as jnp
from jax import lax
from jax.experimental import pallas as pl
from jax.experimental.pallas import tpu as pltpu
from jax.sharding import PartitionSpec as P

MESH = pl.DeviceIdType.MESH
F32 = jnp.float32
BF16 = jnp.bfloat16
NT = (((1,), (1,)), ((), ()))
NN = (((1,), (0,)), ((), ()))
VMEM_LIMIT = 60 * 1024 * 1024
AXES = ("gx", "gy")
SIDES = [(sx, sy) for sx in (-1, 0, 1) for sy in (-1, 0, 1) if (sx, sy) != (0, 0)]


def dot(a, b, dims):
    return lax.dot_general(a, b, dims, preferred_element_type=F32)


def twice(matrix):
    return jnp.concatenate([matrix, matrix], axis=0)


def low_half(shape, rank):
    return lax.broadcasted_iota(jnp.int32, shape, len(shape) - 1) < rank


def pair_columns(wide, vectors, rank):
    pairs = wide.reshape(-1, 2, vectors, 2 * rank)
    even, odd = pairs[:, 0], pairs[:, 1]
    return jnp.where(low_half(even.shape, rank), even, odd).astype(BF16)


def split_columns(paired, rank):
    count, vectors, lanes = paired.shape
    low = low_half((1, lanes), rank).astype(F32).astype(BF16)
    both = jnp.stack([paired * low, paired * (1 - low)], axis=1)
    return both.reshape(count * 2 * vectors, lanes)


def span(side, size, width):
    if side == 0:
        return pl.ds(0, size), pl.ds(width, size)
    if side > 0:
        return pl.ds(size - width, width), pl.ds(0, width)
    return pl.ds(0, width), pl.ds(width + size, width)


def main_kernel(levels, rank, steps, offsets, counts, *refs):
    (samples, codes, listed_counts, codes_upper, counts_upper) = refs[:5]
    (basis, transfer, coupling, near, near_out, leaf_down) = refs[5:11]
    scratch = refs[11:]
    codes_flat, masks, tops, total_near, top_rim, bottom_rim, left_rim, right_rim = scratch[:8]
    send, recv, shifted, top_send, top_recv = scratch[8:13]
    padded = scratch[13 : 13 + levels]
    uppers = scratch[13 + levels : 13 + levels + steps]
    downs = (leaf_down, *scratch[13 + levels + steps :])
    patch, _, vectors, sources = samples.shape
    across, along = counts
    total = across * along
    lanes = 2 * rank
    wide = 36 * rank
    row_index, col_index = lax.axis_index("gx"), lax.axis_index("gy")
    me = row_index * along + col_index

    for rim in (top_rim, bottom_rim, left_rim, right_rim):
        rim[...] = jnp.zeros(rim.shape, BF16)
    for level in range(levels):
        target = padded[level]
        rows, cols = target.shape[:2]
        for spot in (
            (pl.ds(0, 2), pl.ds(0, cols)),
            (pl.ds(rows - 2, 2), pl.ds(0, cols)),
            (pl.ds(2, rows - 4), pl.ds(0, 1)),
            (pl.ds(2, rows - 4), pl.ds(cols - 1, 1)),
        ):
            target[spot[0], spot[1]] = jnp.zeros(
                (spot[0].size, spot[1].size, vectors, lanes), BF16
            )

    def place(device):
        return (device // along, device % along)

    barrier = pltpu.get_barrier_semaphore()

    def greet(step, carry):
        pl.semaphore_signal(
            barrier, inc=1, device_id=place((me + step) % total), device_id_type=MESH
        )
        return carry

    lax.fori_loop(1, total, greet, 0)

    def top_copy(step, sender):
        return pltpu.make_async_remote_copy(
            src_ref=tops.at[row_index, col_index],
            dst_ref=tops.at[sender // along, sender % along],
            send_sem=top_send.at[step],
            recv_sem=top_recv.at[step],
            device_id=place((me + step) % total),
            device_id_type=MESH,
        )

    def coeff_copy(level, number):
        sx, sy = SIDES[number]
        rows_from, rows_to = span(sx, patch >> level, 2)
        cols_from, cols_to = span(sy, patch >> (level + 1), 1)
        rows_from = pl.ds(rows_from.start + 2, rows_from.size)
        cols_from = pl.ds(cols_from.start + 1, cols_from.size)
        return pltpu.make_async_remote_copy(
            src_ref=padded[level].at[rows_from, cols_from],
            dst_ref=padded[level].at[rows_to, cols_to],
            send_sem=send.at[level, number],
            recv_sem=recv.at[level, number],
            device_id=(row_index + sx, col_index + sy),
            device_id_type=MESH,
        )

    half = patch // 2

    def sample_copy(number, late=False):
        sx, sy = SIDES[number]
        rows_from, _ = span(sx, patch, 1)
        cols_from, cols_to = span(sy, patch, 1)
        if sx == 0:
            rim = left_rim if sy > 0 else right_rim
            rows_from = pl.ds(half if late else 0, half)
            spot = rim.at[pl.ds(1 + rows_from.start, half), pl.ds(0, 1)]
        else:
            rim = top_rim if sx > 0 else bottom_rim
            spot = rim.at[pl.ds(0, 1), cols_to]
        return pltpu.make_async_remote_copy(
            src_ref=samples.at[rows_from, cols_from],
            dst_ref=spot,
            send_sem=send.at[levels + late, number],
            recv_sem=recv.at[levels + late, number],
            device_id=(row_index + sx, col_index + sy),
            device_id_type=MESH,
        )

    def inside(sx, sy):
        there_row, there_col = row_index + sx, col_index + sy
        return (there_row >= 0) & (there_row < across) & (there_col >= 0) & (there_col < along)

    slots = codes.shape[-1]
    for level in range(levels):
        size = patch >> level
        for row in range(size):
            begin = (row << level) * patch * levels + level
            listed = codes[pl.ds(begin, size, stride=levels << level), :]
            count = listed_counts[row << level, pl.ds(0, size, stride=1 << level), :]
            used = lax.broadcasted_iota(jnp.int32, (size, slots), 1) < count[:, level : level + 1]
            spot = offsets[level] + row * size
            codes_flat[spot : spot + size, :] = jnp.where(used, listed, -1)
    begin = 0
    for step in range(steps):
        cols = along >> step
        index = begin + (row_index // 2**step) * cols + col_index // 2**step
        used = lax.broadcasted_iota(jnp.int32, (1, slots), 1) < counts_upper[index]
        spot = offsets[levels] + step
        codes_flat[spot : spot + 1, :] = jnp.where(used, codes_upper[pl.ds(index, 1), :], -1)
        begin += (across >> step) * cols
    code_lane = lax.broadcasted_iota(jnp.int32, (128, wide), 1) // rank
    code_row = lax.broadcasted_iota(jnp.int32, (128, wide), 0)
    widen = (code_lane == code_row).astype(F32).astype(BF16)
    group = 64

    def member(number, carry):
        start = pl.multiple_of(number * group, group)
        listed = codes_flat[pl.ds(start, group), :]
        code = lax.broadcasted_iota(jnp.int32, (group, 128), 1)
        found = jnp.zeros((group, 128), F32)
        for slot in range(listed.shape[1]):
            found = jnp.where(listed[:, slot : slot + 1] == code, 1.0, found)
        masks[pl.ds(start, group), :] = dot(found.astype(BF16), widen, NN)
        return carry

    lax.fori_loop(0, masks.shape[0] // group, member, 0)

    pl.semaphore_wait(barrier, total - 1)

    def start_top(step, carry):
        top_copy(step, me).start()
        return carry

    for number, (sx, sy) in enumerate(SIDES):

        @pl.when(inside(sx, sy))
        def _():
            sample_copy(number).start()

    own_basis = twice(basis[...])

    def project(i, carry):
        rows = samples[i].reshape(patch * vectors, sources)
        padded[0][i + 2, 1 : 1 + patch // 2] = pair_columns(
            dot(rows, own_basis, NT), vectors, rank
        )
        return carry

    lax.fori_loop(0, patch, project, 0)
    for level in range(levels):
        child = padded[level]
        matrix = twice(transfer[level])
        cols = patch >> (level + 1)
        for row in range(cols):
            grouped = jnp.concatenate(
                [child[2 * row + 2, 1 : 1 + cols], child[2 * row + 3, 1 : 1 + cols]], axis=-1
            )
            lifted = dot(grouped.reshape(-1, 4 * rank), matrix, NT)
            if level < levels - 1:
                padded[level + 1][row + 2, 1 : 1 + cols // 2] = pair_columns(
                    lifted, vectors, rank
                )
            else:
                odd = col_index % 2
                lane = lax.broadcasted_iota(jnp.int32, lifted.shape, 1)
                own = (lane >= odd * rank) & (lane < (odd + 1) * rank)
                tops[row_index, col_index] = jnp.where(own, lifted, 0.0).astype(BF16)

    lax.fori_loop(1, total, start_top, 0)
    for level in range(levels - 1, -1, -1):
        for number, (sx, sy) in enumerate(SIDES):

            @pl.when(inside(sx, sy))
            def _():
                coeff_copy(level, number).start()

    for number, (sx, sy) in enumerate(SIDES):
        if sx == 0:

            @pl.when(inside(sx, sy))
            def _():
                sample_copy(number, True).start()

    def shift(number, carry):
        level, part = number // coupling.shape[1], number % coupling.shape[1]
        shifted[level, part] = coupling[level, part][:, rank:]
        return carry

    lax.fori_loop(0, coupling.shape[0] * coupling.shape[1], shift, 0)

    def near_row(row, row_steps):
        blank = jnp.zeros((1, vectors, sources), BF16)
        left = []
        for row_step in row_steps:
            line = samples[row + row_step - 1]
            left.append(jnp.concatenate([blank, line[: patch - 1]], axis=0))
            left.append(line)
            left.append(jnp.concatenate([line[1:], blank], axis=0))
        left = jnp.concatenate([part.reshape(-1, sources) for part in left], axis=-1)
        flat = jnp.concatenate(
            [near[3 * row_step + step] for row_step in row_steps for step in range(3)], axis=-1
        )
        total_near[row] = dot(left, flat, NT)

    near_row(0, (1, 2))
    near_row(patch - 1, (0, 1))

    def near_body(row, carry):
        near_row(row, (0, 1, 2))
        return carry

    lax.fori_loop(1, patch - 1, near_body, 0)

    def wait_top(step, carry):
        top_copy(step, (me + total - step) % total).wait_recv()
        return carry

    lax.fori_loop(1, total, wait_top, 0)

    def weights(level, row_bit, col_bit):
        source = coupling if col_bit else shifted
        flat = jnp.concatenate(
            [source[level, code + 1 - row_bit, :, 0 : 6 * rank] for code in range(6)], axis=-1
        )
        return twice(flat)

    def window(ref, row, col):
        return jnp.concatenate(
            [ref[row + code, col + step] for code in range(6) for step in range(3)], axis=-1
        )

    def masked(slab, mask_row):
        mask = jnp.broadcast_to(masks[pl.ds(mask_row, 1), :], (16, wide)).astype(BF16)
        return (slab.reshape(-1, 16, wide) * mask[None]).reshape(slab.shape)

    uppers[0][...] = jnp.zeros(uppers[0].shape, BF16)
    for row in range(across):
        for col in range(along // 2):
            uppers[0][row + 2, col + 1] = tops[row, 2 * col] + tops[row, 2 * col + 1]
    top_matrix = twice(transfer[levels])
    for step in range(steps - 1):
        child, parent = uppers[step], uppers[step + 1]
        parent[...] = jnp.zeros(parent.shape, BF16)
        rows, cols = across >> step, along >> (step + 1)
        for row in range(rows // 2):
            grouped = jnp.concatenate(
                [child[2 * row + 2, 1 : 1 + cols], child[2 * row + 3, 1 : 1 + cols]], axis=-1
            )
            lifted = dot(grouped.reshape(-1, 4 * rank), top_matrix, NT)
            parent[row + 2, 1 : 1 + cols // 2] = pair_columns(lifted, vectors, rank)
    low = low_half((vectors, lanes), rank)
    low_mask = low_half((1, lanes), rank).astype(F32).astype(BF16)
    images = []
    begin = offsets[levels]
    for step in range(steps):
        row, col = row_index // 2**step, col_index // 2**step
        slab = window(uppers[step], 2 * (row // 2), col // 2)
        slab = masked(slab, begin + step)
        bit = row % 2
        image = []
        for source in (shifted, coupling):
            flat = jnp.concatenate(
                [source[levels, code + 1 - bit, :, 0 : 6 * rank] for code in range(6)], axis=-1
            )
            image.append(dot(slab, twice(flat), NT))
        images.append(jnp.where(col % 2 == 0, image[0], image[1]))
    down = images[-1]
    for step in range(steps - 2, -1, -1):
        row, col = row_index // 2**step, col_index // 2**step
        carried = dot(down.astype(BF16) * low_mask, top_matrix, NN)
        part = jnp.where(row % 2 == 0, carried[:, :lanes], carried[:, lanes:])
        turned = pltpu.roll(part, rank, 1)
        part = jnp.where(low == (col % 2 == 0), part, turned)
        down = images[step] + part
    spread_top = down.astype(BF16) * low_mask

    def level_rows(level, rows):
        size = patch >> level
        if level == levels - 1:
            parent = spread_top
        else:
            parent = jnp.concatenate(
                [split_columns(downs[level + 1][row], rank) for row in rows], axis=0
            )
        carried = dot(parent, twice(transfer[level]), NN)
        slabs = [
            (row, col, window(padded[level], 2 * row, col))
            for row in rows
            for col in range(size // 2)
        ]
        for row_bit in range(2):
            image = []
            for col_bit in range(2):
                left = jnp.concatenate(
                    [
                        masked(
                            slab, offsets[level] + (2 * row + row_bit) * size + col_bit + 2 * col
                        )
                        for row, col, slab in slabs
                    ],
                    axis=0,
                )
                image.append(dot(left, weights(level, row_bit, col_bit), NT))
            summed = jnp.where(low_half(image[0].shape, rank), image[0], image[1])
            summed = summed + carried[:, row_bit * lanes : (row_bit + 1) * lanes]
            summed = summed.astype(BF16).reshape(len(rows), -1, vectors, lanes)
            for number, row in enumerate(rows):
                downs[level][2 * row + row_bit] = summed[number]

    for level in range(levels - 1, -1, -1):
        for number, (sx, sy) in enumerate(SIDES):

            @pl.when(inside(-sx, -sy))
            def _():
                coeff_copy(level, number).wait_recv()

        count = patch >> (level + 1)
        if count <= 2:
            level_rows(level, list(range(count)))
        else:

            def body(pair, carry, level=level):
                level_rows(level, [2 * pair, 2 * pair + 1])
                return carry

            lax.fori_loop(0, count // 2, body, 0)

    for number, (sx, sy) in enumerate(SIDES):

        @pl.when(inside(-sx, -sy))
        def _():
            sample_copy(number).wait_recv()
            if sx == 0:
                sample_copy(number, True).wait_recv()

    for rim, column, step in ((left_rim, 0, 0), (right_rim, patch - 1, 2)):
        left = jnp.concatenate(
            [rim[part : part + patch, 0].reshape(-1, sources) for part in range(3)], axis=-1
        )
        flat = jnp.concatenate([near[3 * part + step] for part in range(3)], axis=-1)
        extra = dot(left, flat, NT).reshape(patch, vectors, sources)
        spot = pl.ds(column * vectors, vectors)
        total_near[:, spot, :] = total_near[:, spot, :] + extra
    for rim, row, step in ((top_rim, 0, 0), (bottom_rim, patch - 1, 6)):
        left = jnp.concatenate(
            [rim[0, part : part + patch].reshape(-1, sources) for part in range(3)], axis=-1
        )
        flat = jnp.concatenate([near[step + part] for part in range(3)], axis=-1)
        total_near[row] = total_near[row] + dot(left, flat, NT)
    def round_row(row, carry):
        near_out[row] = total_near[row].astype(BF16)
        return carry

    lax.fori_loop(0, patch, round_row, 0)

    for number, (sx, sy) in enumerate(SIDES):

        @pl.when(inside(sx, sy))
        def _():
            for level in range(levels):
                coeff_copy(level, number).wait_send()
            sample_copy(number).wait_send()
            if sx == 0:
                sample_copy(number, True).wait_send()

    def sent_top(step, carry):
        top_copy(step, me).wait_send()
        return carry

    lax.fori_loop(1, total, sent_top, 0)


def finish_kernel(rank, near_sum, leaf_down, basis, out):
    rows, patch, vectors, sources = out.shape
    basis2 = twice(basis[...])
    for row in range(rows):
        summed = near_sum[row].astype(F32) + dot(split_columns(leaf_down[row], rank), basis2, NN)
        out[row] = summed.astype(BF16).reshape(patch, vectors, sources)


def shards(
    samples,
    leaf_basis,
    transfer,
    coupling,
    near_tiles,
    codes_local,
    counts_local,
    codes_upper,
    counts_upper,
):
    patch, _, vectors, sources = samples.shape
    rank = leaf_basis.shape[0]
    levels = transfer.shape[0] - 1
    lanes = 2 * rank
    across, along = lax.axis_size("gx"), lax.axis_size("gy")
    steps = 1
    while across >> steps >= 2:
        steps += 1
    vmem = pl.BlockSpec(memory_space=pltpu.VMEM)

    shapes = [
        jax.ShapeDtypeStruct((patch >> level, patch >> (level + 1), vectors, lanes), BF16)
        for level in range(levels)
    ]
    offsets = [0]
    for level in range(levels):
        offsets.append(offsets[-1] + (patch >> level) ** 2)
    rows = offsets[-1] + steps
    rows = (rows + 63) // 64 * 64
    near_sum, leaf_down = pl.pallas_call(
        functools.partial(main_kernel, levels, rank, steps, offsets, (across, along)),
        out_shape=[
            jax.ShapeDtypeStruct((patch, patch * vectors, sources), BF16),
            shapes[0],
        ],
        in_specs=[vmem] * 4 + [pl.BlockSpec(memory_space=pltpu.SMEM)] + [vmem] * 4,
        out_specs=[vmem, vmem],
        scratch_shapes=[
            pltpu.VMEM((rows, codes_local.shape[-1]), jnp.int32),
            pltpu.VMEM((rows, 36 * rank), F32),
            pltpu.VMEM((across, along, vectors, lanes), BF16),
            pltpu.VMEM((patch, patch * vectors, sources), F32),
            pltpu.VMEM((1, patch + 2, vectors, sources), BF16),
            pltpu.VMEM((1, patch + 2, vectors, sources), BF16),
            pltpu.VMEM((patch + 2, 1, vectors, sources), BF16),
            pltpu.VMEM((patch + 2, 1, vectors, sources), BF16),
            pltpu.SemaphoreType.DMA((levels + 2, len(SIDES))),
            pltpu.SemaphoreType.DMA((levels + 2, len(SIDES))),
            pltpu.VMEM(coupling.shape[:3] + (6 * rank,), BF16),
            pltpu.SemaphoreType.DMA((across * along,)),
            pltpu.SemaphoreType.DMA((across * along,)),
        ]
        + [
            pltpu.VMEM((shape.shape[0] + 4, shape.shape[1] + 2, vectors, lanes), BF16)
            for shape in shapes[:levels]
        ]
        + [
            pltpu.VMEM(((across >> step) + 4, (along >> (step + 1)) + 2, vectors, lanes), BF16)
            for step in range(steps)
        ]
        + [pltpu.VMEM(shape.shape, BF16) for shape in shapes[1:levels]],
        compiler_params=pltpu.CompilerParams(
            collective_id=0, has_side_effects=True, vmem_limit_bytes=VMEM_LIMIT
        ),
        name="main",
    )(
        samples,
        codes_local.reshape(-1, codes_local.shape[-1]),
        counts_local,
        codes_upper,
        counts_upper,
        leaf_basis,
        transfer,
        coupling,
        near_tiles,
    )
    strip = patch // 4
    return pl.pallas_call(
        functools.partial(finish_kernel, rank),
        out_shape=jax.ShapeDtypeStruct(samples.shape, BF16),
        grid=(patch // strip,),
        in_specs=[
            pl.BlockSpec((strip, patch * vectors, sources), lambda i: (i, 0, 0)),
            pl.BlockSpec((strip, patch // 2, vectors, lanes), lambda i: (i, 0, 0, 0)),
            pl.BlockSpec((rank, sources), lambda i: (0, 0)),
        ],
        out_specs=pl.BlockSpec((strip, patch, vectors, sources), lambda i: (i, 0, 0, 0)),
        name="finish",
    )(near_sum, leaf_down, leaf_basis)


def solution(mesh):
    placed = (
        P("gx", "gy", None, None),
        P(),
        P(),
        P(),
        P(),
        P("gx", "gy", None, None),
        P("gx", "gy", None),
        P(),
        P(),
    )
    return jax.shard_map(
        shards, mesh=mesh, in_specs=placed, out_specs=P("gx", "gy", None, None), check_vma=False
    )
```
